32 devices in a mesh: groups: 2 (over x), tensor: 4 (over y, core), dp: 4 (over z).
Axes of the slice: x: 2, y: 2, z: 4, core: 2. Of those that a mesh axis runs over, the one named last changes fastest.
Arguments:
- hidden_in: bfloat16 [1024, 8192], P(('groups', 'dp'), 'tensor'), parts along dimension 0, may hold values from -6 to 6
- out_grad: bfloat16 [1024, 8192], P(('groups', 'dp'), 'tensor'), parts along dimension 0, may hold values from -6 to 6
- w_gate_up: bfloat16 [2, 28672, 8192], P(None, ('tensor', 'dp')), may hold values from -0.0625 to 0.0625
- w_down: bfloat16 [28672, 8192], P(('tensor', 'dp')), may hold values from -0.03125 to 0.03125
- feat_proj: bfloat16 [8192, 192], P('tensor'), may hold values from -0.0625 to 0.0625
- unit_proj: bfloat16 [28672, 192], P(('tensor', 'dp')), may hold values from -0.03125 to 0.03125
- precond: float32 [3, 4096, 4096], P(None, ('tensor', 'dp')), may hold values from -20 to 20
Outputs:
- precond_grad: float32 [3, 8, 4096], P(None, 'groups', ('tensor', 'dp')), parts along dimension 1
The draws below stay inside these ranges and needn't reach their ends.
There are 2 independent parts, one for each index of `groups`. The reference program is written for one: setup_inputs(seed, part) draws one part's arguments, and reference() takes and returns one part's arrays. A program takes and returns all parts, laid end to end along the dimension named above; an argument that names none is the same for every part. Nothing has to cross between parts.
All inputs are finite; a program needn't handle non-finite values.
Results may differ from the reference program's by a relative error of at most 0.0029.
Values may be sent and summed in bfloat16 or wider, within the bound.
No kernel may reach another device: no remote copies, remote signals or barrier semaphores. Data moves between devices by JAX's collectives and lax.ppermute only.
A program may use at most 256 MiB of HBM per device.

```python
import math
import jax
import jax.numpy as jnp
from jax import lax

D = 8192
FF = 28672
K = 64
SEQ = 128
SEQS = 4
TOKENS = 512


def draw_precond(key, part):
    off_key, diag_key = jax.random.split(key, 2)
    mat_order = K * K
    normal_draw = jax.random.normal(off_key, (3, mat_order, mat_order), jnp.float32)
    symmetric = (normal_draw + jnp.swapaxes(normal_draw, 1, 2)) * (0.5 / math.sqrt(2.0 * mat_order))
    row_ids = lax.broadcasted_iota(jnp.int32, (mat_order, mat_order), 0)
    col_ids = lax.broadcasted_iota(jnp.int32, (mat_order, mat_order), 1)
    identity = (row_ids == col_ids).astype(jnp.float32)
    diagonal = jax.random.uniform(diag_key, (3, mat_order, 1), jnp.float32, 1.0, 2.0)
    matrix = symmetric + identity[None, :, :] * diagonal
    return matrix


def shard_levels(stream_key, dims, cuts, low, high):
    def one(position, shards_of):
        steps = jax.random.uniform(jax.random.fold_in(jax.random.fold_in(stream_key, 6), position), (shards_of,), jnp.float32, low / len(cuts), high / len(cuts))
        return jnp.repeat(jnp.exp(steps), dims[position] // shards_of).reshape((-1,) + (1,) * (len(dims) - position - 1))

    factor_of = one(*cuts[0])
    for cut in cuts[1:]:
        factor_of = factor_of * one(*cut)
    return factor_of


def scatter_about(stream_key, shape, width, limit, pieces=(), held_as=jnp.bfloat16):
    drawn = jax.random.normal(stream_key, shape, jnp.float32) * width
    if len(pieces) > 0:
        drawn = shard_levels(stream_key, shape, pieces, -0.22, 0.18) * drawn
    return jnp.clip(drawn, min=-limit, max=limit).astype(held_as)


def setup_inputs(seed: int = 0, part: int = 0) -> dict:
    seeds = jax.random.split(jax.random.key(seed), 8)
    part_splits = jax.random.split(jax.random.fold_in(seeds[7], part), 8)
    hidden_in = scatter_about(part_splits[0], (TOKENS, D), 1.0, 6.0, ((0, 4), (1, 4)))
    out_grad = scatter_about(part_splits[1], (TOKENS, D), 1.0, 6.0, ((0, 4), (1, 4)))
    w_gate_up = scatter_about(seeds[2], (2, FF, D), D ** -0.5, 0.0625, ((1, 16),))
    w_down = scatter_about(seeds[3], (FF, D), FF ** -0.5, 0.03125, ((0, 16),))
    feat_proj = scatter_about(seeds[4], (D, 3 * K), D ** -0.5, 0.0625, ((0, 4),))
    unit_proj = scatter_about(seeds[5], (FF, 3 * K), FF ** -0.5, 0.03125, ((0, 16),))
    precond = draw_precond(jax.random.fold_in(seeds[7], 71), part)
    return dict(hidden_in=hidden_in, out_grad=out_grad, w_gate_up=w_gate_up, w_down=w_down, feat_proj=feat_proj, unit_proj=unit_proj, precond=precond)


def form_sketch(in_side, out_side):
    left_rows = in_side.reshape(SEQS, SEQ, 3, K)
    right_rows = out_side.reshape(SEQS, SEQ, 3, K)
    sketch = jnp.einsum("stwi,stwj->wsij", left_rows, right_rows, precision=lax.Precision.HIGHEST)
    sketch = sketch * (SEQ ** -0.5)
    return sketch.reshape(3, SEQS, K * K)


def reference(hidden_in, out_grad, w_gate_up, w_down, feat_proj, unit_proj, precond):
    contract_last = (((1,), (1,)), ((), ()))
    gate_pre = lax.dot_general(hidden_in, w_gate_up[0], contract_last, preferred_element_type=jnp.float32)
    up_pre = lax.dot_general(hidden_in, w_gate_up[1], contract_last, preferred_element_type=jnp.float32)
    hid_grad = lax.dot_general(out_grad, w_down, contract_last, preferred_element_type=jnp.float32)
    gate_sig = jax.nn.sigmoid(gate_pre)
    silu_gate = gate_pre * gate_sig
    hidden = (silu_gate * up_pre).astype(jnp.bfloat16)
    gate_grad = (hid_grad * up_pre * gate_sig * (1.0 + gate_pre * (1.0 - gate_sig))).astype(jnp.bfloat16)
    up_grad = (hid_grad * silu_gate).astype(jnp.bfloat16)
    feat_side = jnp.concatenate([
        jnp.dot(hidden_in, feat_proj[:, :2 * K], preferred_element_type=jnp.float32),
        jnp.dot(out_grad, feat_proj[:, 2 * K:], preferred_element_type=jnp.float32)], axis=1)
    unit_side = jnp.concatenate([
        jnp.dot(gate_grad, unit_proj[:, :K], preferred_element_type=jnp.float32),
        jnp.dot(up_grad, unit_proj[:, K:2 * K], preferred_element_type=jnp.float32),
        jnp.dot(hidden, unit_proj[:, 2 * K:], preferred_element_type=jnp.float32)], axis=1)
    in_side = jnp.concatenate([feat_side[:, :2 * K], unit_side[:, 2 * K:]], axis=1)
    out_side = jnp.concatenate([unit_side[:, :2 * K], feat_side[:, 2 * K:]], axis=1)
    sketch = form_sketch(in_side, out_side)
    return jnp.einsum("wrc,wsc->wsr", precond, sketch, precision=lax.Precision.HIGHEST)
```

```python
import functools

import jax
import jax.numpy as jnp
from jax import lax
from jax.experimental import pallas as pl
from jax.experimental.pallas import tpu as pltpu
from jax.sharding import PartitionSpec as P

K = 64
SEQ = 128
BOTH = ("tensor", "dp")
NT = (((1,), (1,)), ((), ()))
MIB = 1 << 20


def project_pair(rows_in, rows_out, columns):
    return jnp.concatenate(
        [
            jnp.dot(rows_in, columns[:, : 2 * K], preferred_element_type=jnp.float32),
            jnp.dot(rows_out, columns[:, 2 * K :], preferred_element_type=jnp.float32),
        ],
        axis=1,
    )


def form_sketch(in_side, out_side):
    seq_count = in_side.shape[0] // SEQ
    left_rows = in_side.reshape(seq_count, SEQ, 3, K)
    right_rows = out_side.reshape(seq_count, SEQ, 3, K)
    sketch = jnp.einsum("stwi,stwj->wsij", left_rows, right_rows, precision=lax.Precision.HIGHEST)
    sketch = sketch * SEQ ** (-0.5)
    return sketch.reshape(3, seq_count, K * K)


def activations(gate_pre, up_pre, hid_grad):
    gate_sig = jax.nn.sigmoid(gate_pre)
    silu_gate = gate_pre * gate_sig
    hidden = (silu_gate * up_pre).astype(jnp.bfloat16)
    gate_grad = (hid_grad * up_pre * gate_sig * (1.0 + gate_pre * (1.0 - gate_sig))).astype(
        jnp.bfloat16
    )
    up_grad = (hid_grad * silu_gate).astype(jnp.bfloat16)
    return gate_grad, up_grad, hidden


def local_plain(hidden_in, out_grad, w_gate_up, w_down, feat_proj, unit_proj, precond):
    unit_width, model_width = w_down.shape
    w_both = w_gate_up.reshape(2 * unit_width, model_width)
    paired = jnp.stack([hidden_in, out_grad])
    columns = lax.all_gather(feat_proj, "tensor", axis=0, tiled=True)
    rows_all = lax.all_gather(paired, "dp", axis=1, tiled=True)
    pieces = lax.all_gather(rows_all, "tensor", axis=2, tiled=True)
    pre_act = lax.dot_general(pieces[0], w_both, NT, preferred_element_type=jnp.float32)
    hid_grad = lax.dot_general(pieces[1], w_down, NT, preferred_element_type=jnp.float32)
    feat_side = project_pair(pieces[0], pieces[1], columns)
    sides = activations(pre_act[:, :unit_width], pre_act[:, unit_width:], hid_grad)
    unit_part = jnp.concatenate(
        [
            jnp.dot(side, unit_proj[:, n * K : (n + 1) * K], preferred_element_type=jnp.float32)
            for n, side in enumerate(sides)
        ],
        axis=1,
    )
    unit_side = lax.psum(unit_part, BOTH)
    in_side = jnp.concatenate([feat_side[:, : 2 * K], unit_side[:, 2 * K :]], axis=1)
    out_side = jnp.concatenate([unit_side[:, : 2 * K], feat_side[:, 2 * K :]], axis=1)
    sketch = form_sketch(in_side, out_side)
    return jnp.einsum("wrc,wsc->wsr", precond, sketch, precision=lax.Precision.HIGHEST)


TENSOR = 4
ROWS = 4


def swap_with(flip):
    return [(t * ROWS + z, (t ^ flip) * ROWS + z) for t in range(TENSOR) for z in range(ROWS)]


def shift_rows(step, wrap=True):
    return [
        (t * ROWS + z, t * ROWS + (z + step) % ROWS)
        for t in range(TENSOR)
        for z in range(ROWS)
        if wrap or 0 <= z + step < ROWS
    ]


def send(value, pairs):
    return lax.ppermute(value, BOTH, pairs)


FORWARD = [(t * ROWS + a, t * ROWS + b) for t in range(TENSOR) for a, b in ((2, 3), (1, 0))]


def gather_rows(own):
    row = lax.axis_index("dp")
    from_1 = send(own, shift_rows(1, False))
    from_2 = send(own, shift_rows(2))
    from_3 = send(own, shift_rows(-1, False))
    end = send(from_2, FORWARD)
    from_1 = jnp.where(row == 0, end, from_1)
    from_3 = jnp.where(row == ROWS - 1, end, from_3)
    return jnp.concatenate([from_1, from_2, from_3], axis=1)


def matmul_kernel(blocks, tokens, first, last, *refs):
    count = len(blocks)
    refs = list(refs)
    where_ref = refs.pop(0)
    arrays = [(refs.pop(0), refs.pop(0)) for _ in range(count)]
    gate_up = [refs.pop(0) for _ in range(count)]
    down = [refs.pop(0) for _ in range(count)]
    acc_in = None if first else refs.pop(0)
    if last:
        proj_ref = refs.pop(0)
        mine_ref, theirs_ref = refs.pop(0), refs.pop(0)
    else:
        acc_out = refs.pop(0)
    rows = [refs.pop(0) for _ in range(count)]
    sems = refs.pop(0)
    step = pl.program_id(0)

    @pl.when(step == 0)
    def _():
        copies = []
        for n, (block, (own, rest)) in enumerate(zip(blocks, arrays)):
            _, offset, width, lead = block
            split = own.shape[1]
            copies.append(
                pltpu.make_async_copy(
                    own.at[:, :, pl.ds(offset, width)], rows[n].at[:, pl.ds(0, split), :], sems.at[2 * n]
                )
            )
            copies.append(
                pltpu.make_async_copy(
                    rest.at[pl.ds(lead, 2)],
                    rows[n].at[:, pl.ds(split, tokens - split), :],
                    sems.at[2 * n + 1],
                )
            )
        for copy in copies:
            copy.start()
        for copy in copies:
            copy.wait()
        if last:
            ut_ref = refs[0]
            ut_ref[...] = jnp.zeros_like(ut_ref)

    def total(which):
        value = None if first else acc_in[0, which]
        for n in range(count):
            weight = down[n][...] if which == 2 else gate_up[n][which]
            part = lax.dot_general(
                rows[n][1 if which == 2 else 0], weight, NT, preferred_element_type=jnp.float32
            )
            value = part if value is None else value + part
        return value

    if not last:
        for which in range(3):
            acc_out[0, which] = total(which)
        return
    ut_ref = refs[0]
    sides = activations(total(0), total(1), total(2))
    for n, side in enumerate(sides):
        ut_ref[pl.ds(n * K, K), :] += lax.dot_general(
            proj_ref[pl.ds(n * K, K), :], side, NT, preferred_element_type=jnp.float32
        )

    @pl.when(step == pl.num_programs(0) - 1)
    def _():
        half = mine_ref.shape[0]
        core = lax.rem(where_ref[0], 2)
        mine_ref[...] = ut_ref[pl.ds(pl.multiple_of(core * half, 8), half), :]
        theirs_ref[...] = ut_ref[pl.ds(pl.multiple_of((1 - core) * half, 8), half), :]


def matmul_step(where, blocks, arrays, w_gate_up, w_down, acc, unit_proj_t=None):
    first, last = acc is None, unit_proj_t is not None
    unit_width, model_width = w_down.shape
    own_width = model_width // TENSOR
    tokens = arrays[0][0].shape[1] + arrays[0][1].shape[1]
    tile = 256
    tiles = unit_width // tile

    def at(owner, offset, width):
        per = own_width // width
        return lambda i, at_ref: at_ref[owner] * per + offset // width

    in_specs = [pl.BlockSpec(memory_space=pl.ANY)] * (2 * len(blocks))
    operands = [a for pair in arrays for a in pair]
    for owner, offset, width, _ in blocks:
        column = at(owner, offset, width)
        in_specs.append(pl.BlockSpec((2, tile, width), lambda i, r, c=column: (0, i, c(i, r))))
        operands.append(w_gate_up)
    for owner, offset, width, _ in blocks:
        column = at(owner, offset, width)
        in_specs.append(pl.BlockSpec((tile, width), lambda i, r, c=column: (i, c(i, r))))
        operands.append(w_down)
    acc_spec = pl.BlockSpec((1, 3, tokens, tile), lambda i, r: (i, 0, 0, 0))
    acc_shape = jax.ShapeDtypeStruct((tiles, 3, tokens, tile), jnp.float32)
    aliases = {}
    if not first:
        if not last:
            aliases = {1 + len(operands): 0}
        in_specs.append(acc_spec)
        operands.append(acc)
    scratch = [pltpu.VMEM((2, tokens, width), jnp.bfloat16) for _, _, width, _ in blocks]
    scratch.append(pltpu.SemaphoreType.DMA((2 * len(blocks),)))
    if last:
        in_specs.append(pl.BlockSpec((3 * K, tile), lambda i, r: (0, i)))
        operands.append(unit_proj_t)
        half = jax.ShapeDtypeStruct((3 * K // 2, tokens), jnp.float32)
        out_shape = (half, half)
        out_specs = (pl.BlockSpec(half.shape, lambda i, r: (0, 0)),) * 2
        scratch.append(pltpu.VMEM((3 * K, tokens), jnp.float32))
    else:
        out_shape, out_specs = acc_shape, acc_spec
    depth = sum(width for _, _, width, _ in blocks)
    return pl.pallas_call(
        functools.partial(matmul_kernel, blocks, tokens, first, last),
        out_shape=out_shape,
        grid_spec=pltpu.PrefetchScalarGridSpec(
            num_scalar_prefetch=1,
            grid=(tiles,),
            in_specs=in_specs,
            out_specs=out_specs,
            scratch_shapes=scratch,
        ),
        input_output_aliases=aliases,
        compiler_params=pltpu.CompilerParams(vmem_limit_bytes=44 * MIB),
        cost_estimate=pl.CostEstimate(
            flops=2 * tokens * 3 * unit_width * depth,
            bytes_accessed=3 * unit_width * depth * 2 + 4 * depth * tokens,
            transcendentals=0,
        ),
        name="matmul",
    )(where, *operands)


def sketch_kernel(where_ref, feat_ref, mine_ref, other_ref, out_ref, unit_ref):
    half = mine_ref.shape[0]
    core = lax.rem(where_ref[0], 2)
    unit_ref[pl.ds(pl.multiple_of(core * half, 8), half), :] = mine_ref[...]
    unit_ref[pl.ds(pl.multiple_of((1 - core) * half, 8), half), :] = other_ref[...]
    for w in range(3):
        in_ref, side_ref = (feat_ref, unit_ref) if w < 2 else (unit_ref, feat_ref)
        right = side_ref[pl.ds(w * K, K), :]
        parts = [
            lax.dot_general(
                in_ref[pl.ds(w * K + odd, K // 2, stride=2), :],
                right,
                NT,
                precision=lax.Precision.HIGHEST,
                preferred_element_type=jnp.float32,
            )
            for odd in range(2)
        ]
        out_ref[w] = jnp.concatenate(parts, axis=1) * SEQ ** (-0.5)


def sketch_own(where, feat_t, mine, other):
    whole = pl.BlockSpec(memory_space=pltpu.VMEM)
    return pl.pallas_call(
        sketch_kernel,
        out_shape=jax.ShapeDtypeStruct((3, K // 2, 2 * K), jnp.float32),
        in_specs=[pl.BlockSpec(memory_space=pltpu.SMEM), whole, whole, whole],
        out_specs=whole,
        scratch_shapes=[pltpu.VMEM((3 * K, SEQ), jnp.float32)],
        name="sketch",
    )(where, feat_t, mine, other)


def precond_kernel(row_ref, p_ref, *refs):
    sketches, out_ref, sums = refs[:ROWS], refs[ROWS], refs[ROWS + 1]
    height = p_ref.shape[1]
    lanes = 2 * K
    group = 32
    ones = jnp.ones((8, lanes), jnp.float32)

    @pl.loop(0, height // group)
    def _(g):
        at = pl.ds(pl.multiple_of(g * group, group), group)
        totals = [jnp.zeros((group, lanes), jnp.float32) for _ in range(ROWS)]
        for q in range(K // 2):
            part = p_ref[0, at, pl.ds(q * lanes, lanes)]
            for n in range(ROWS):
                totals[n] = totals[n] + part * sketches[n][0, pl.ds(q, 1), :]
        for n in range(ROWS):
            sums[n, at, :] = totals[n]

    for n in range(ROWS):
        seq = lax.rem(row_ref[0] - n + ROWS, ROWS)
        line = lax.dot_general(
            ones,
            sums[n],
            NT,
            precision=lax.Precision.HIGHEST,
            preferred_element_type=jnp.float32,
        )
        out_ref[0, pl.ds(seq, 1), :] = line[:1]


def apply_precond(row, precond, sketches):
    height, order = precond.shape[1:]
    piece = pl.BlockSpec((1, K // 2, 2 * K), lambda w, r: (w, 0, 0))
    return pl.pallas_call(
        precond_kernel,
        out_shape=jax.ShapeDtypeStruct((3, ROWS, height), jnp.float32),
        grid_spec=pltpu.PrefetchScalarGridSpec(
            num_scalar_prefetch=1,
            grid=(3,),
            in_specs=[pl.BlockSpec((1, height, order), lambda w, r: (w, 0, 0))] + [piece] * ROWS,
            out_specs=pl.BlockSpec((1, ROWS, height), lambda w, r: (w, 0, 0)),
            scratch_shapes=[pltpu.VMEM((ROWS, height, 2 * K), jnp.float32)],
        ),
        compiler_params=pltpu.CompilerParams(vmem_limit_bytes=24 * MIB),
        name="precond",
    )(row, precond, *sketches)


CHUNKS = (1024, 512, 256)
A, C, Y, D = range(4)


def local_split(hidden_in, out_grad, w_gate_up, w_down, feat_proj, unit_proj, precond):
    tensor, row = lax.axis_index("tensor"), lax.axis_index("dp")
    where = jnp.stack([tensor, tensor ^ 1, tensor ^ 2, tensor ^ 3]).astype(jnp.int32)
    own = jnp.stack([hidden_in, out_grad])
    width = own.shape[2]
    other_y = send(own, swap_with(2))
    other_core = send(own, swap_with(1))
    other_both = send(other_y, swap_with(1))
    unit_proj_t = unit_proj.T

    feat_t = jnp.concatenate(
        [
            lax.dot_general(
                feat_proj[:, : 2 * K], hidden_in, (((0,), (1,)), ((), ())), preferred_element_type=jnp.float32
            ),
            lax.dot_general(
                feat_proj[:, 2 * K :], out_grad, (((0,), (1,)), ((), ())), preferred_element_type=jnp.float32
            ),
        ],
        axis=0,
    )
    feat_t = feat_t + send(feat_t, swap_with(1))
    feat_t = feat_t + send(feat_t, swap_with(2))

    acc = None
    waiting = ([], [])
    offset = 0
    for size in CHUNKS:
        rest = gather_rows(own[:, :, offset : offset + size])
        rest_core = send(rest, swap_with(1))
        rest_y = send(rest, swap_with(2))
        rest_both = send(rest_y, swap_with(1))
        blocks = waiting[0] + [(A, offset, size, 0), (C, offset, size, 0)]
        arrays = waiting[1] + [(own, rest), (other_core, rest_core)]
        acc = matmul_step(where, blocks, arrays, w_gate_up, w_down, acc)
        waiting = (
            [(Y, offset, size, 0), (D, offset, size, 0)],
            [(other_y, rest_y), (other_both, rest_both)],
        )
        offset += size
    acc = matmul_step(where, *waiting, w_gate_up, w_down, acc)
    size = width - offset
    both = jnp.concatenate([own[:, :, offset:], other_y[:, :, offset:]], axis=0)
    rest = gather_rows(both)
    rest_core = send(rest, swap_with(1))
    blocks = [(A, offset, size, 0), (Y, offset, size, 2), (C, offset, size, 0), (D, offset, size, 2)]
    arrays = [(own, rest), (other_y, rest), (other_core, rest_core), (other_both, rest_core)]
    mine, theirs = matmul_step(where, blocks, arrays, w_gate_up, w_down, acc, unit_proj_t)

    mine = mine + send(theirs, swap_with(1))
    part = mine[:, :SEQ]
    for n in range(1, ROWS):
        part = part + send(mine[:, n * SEQ : (n + 1) * SEQ], shift_rows(-n))
    part = part + send(part, swap_with(2))
    other = send(part, swap_with(1))
    sketch = sketch_own(where, feat_t, part, other)
    sketches = [sketch] + [send(sketch, shift_rows(n)) for n in range(1, ROWS)]
    return apply_precond(row.astype(jnp.int32).reshape(1), precond, sketches)


def local(hidden_in, out_grad, w_gate_up, w_down, feat_proj, unit_proj, precond):
    fits = (
        lax.axis_size("tensor") == TENSOR
        and lax.axis_size("dp") == ROWS
        and hidden_in.shape[0] == SEQ
        and w_down.shape[0] % 256 == 0
        and hidden_in.shape[1] == 2048
    )
    step = local_split if fits else local_plain
    return step(hidden_in, out_grad, w_gate_up, w_down, feat_proj, unit_proj, precond)


def solution(mesh):
    in_specs = (
        P(("groups", "dp"), "tensor"),
        P(("groups", "dp"), "tensor"),
        P(None, ("tensor", "dp"), None),
        P(("tensor", "dp"), None),
        P("tensor", None),
        P(("tensor", "dp"), None),
        P(None, ("tensor", "dp"), None),
    )
    out_specs = P(None, "groups", ("tensor", "dp"))
    return jax.shard_map(local, mesh=mesh, in_specs=in_specs, out_specs=out_specs, check_vma=False)
```

```python
import functools

import jax
import jax.numpy as jnp
from jax import lax
from jax.experimental import pallas as pl
from jax.experimental.pallas import tpu as pltpu
from jax.sharding import PartitionSpec as P

K = 64
SEQ = 128
BOTH = ("tensor", "dp")
NT = (((1,), (1,)), ((), ()))
MIB = 1 << 20


def project_pair(rows_in, rows_out, columns):
    return jnp.concatenate(
        [
            jnp.dot(rows_in, columns[:, : 2 * K], preferred_element_type=jnp.float32),
            jnp.dot(rows_out, columns[:, 2 * K :], preferred_element_type=jnp.float32),
        ],
        axis=1,
    )


def form_sketch(in_side, out_side):
    seq_count = in_side.shape[0] // SEQ
    left_rows = in_side.reshape(seq_count, SEQ, 3, K)
    right_rows = out_side.reshape(seq_count, SEQ, 3, K)
    sketch = jnp.einsum("stwi,stwj->wsij", left_rows, right_rows, precision=lax.Precision.HIGHEST)
    sketch = sketch * SEQ ** (-0.5)
    return sketch.reshape(3, seq_count, K * K)


def activations(gate_pre, up_pre, hid_grad):
    gate_sig = jax.nn.sigmoid(gate_pre)
    silu_gate = gate_pre * gate_sig
    hidden = (silu_gate * up_pre).astype(jnp.bfloat16)
    gate_grad = (hid_grad * up_pre * gate_sig * (1.0 + gate_pre * (1.0 - gate_sig))).astype(
        jnp.bfloat16
    )
    up_grad = (hid_grad * silu_gate).astype(jnp.bfloat16)
    return gate_grad, up_grad, hidden


def local_plain(hidden_in, out_grad, w_gate_up, w_down, feat_proj, unit_proj, precond):
    unit_width, model_width = w_down.shape
    w_both = w_gate_up.reshape(2 * unit_width, model_width)
    paired = jnp.stack([hidden_in, out_grad])
    columns = lax.all_gather(feat_proj, "tensor", axis=0, tiled=True)
    rows_all = lax.all_gather(paired, "dp", axis=1, tiled=True)
    pieces = lax.all_gather(rows_all, "tensor", axis=2, tiled=True)
    pre_act = lax.dot_general(pieces[0], w_both, NT, preferred_element_type=jnp.float32)
    hid_grad = lax.dot_general(pieces[1], w_down, NT, preferred_element_type=jnp.float32)
    feat_side = project_pair(pieces[0], pieces[1], columns)
    sides = activations(pre_act[:, :unit_width], pre_act[:, unit_width:], hid_grad)
    unit_part = jnp.concatenate(
        [
            jnp.dot(side, unit_proj[:, n * K : (n + 1) * K], preferred_element_type=jnp.float32)
            for n, side in enumerate(sides)
        ],
        axis=1,
    )
    unit_side = lax.psum(unit_part, BOTH)
    in_side = jnp.concatenate([feat_side[:, : 2 * K], unit_side[:, 2 * K :]], axis=1)
    out_side = jnp.concatenate([unit_side[:, : 2 * K], feat_side[:, 2 * K :]], axis=1)
    sketch = form_sketch(in_side, out_side)
    return jnp.einsum("wrc,wsc->wsr", precond, sketch, precision=lax.Precision.HIGHEST)


TENSOR = 4
ROWS = 4


def swap_with(flip):
    return [(t * ROWS + z, (t ^ flip) * ROWS + z) for t in range(TENSOR) for z in range(ROWS)]


def swap_rows(flip):
    return [(t * ROWS + z, t * ROWS + (z ^ flip)) for t in range(TENSOR) for z in range(ROWS)]


def send(value, pairs):
    return lax.ppermute(value, BOTH, pairs)


def matmul_kernel(count, last, *refs):
    refs = list(refs)
    where_ref = refs.pop(0)
    pieces = [(refs.pop(0), refs.pop(0)) for _ in range(count)]
    gate_up = [refs.pop(0) for _ in range(count)]
    down = [refs.pop(0) for _ in range(count)]
    if last:
        acc_in, proj_ref, mine_ref, theirs_ref = (refs.pop(0) for _ in range(4))
    else:
        acc_out = refs.pop(0)
    rows = [refs.pop(0) for _ in range(count)]
    sems = refs.pop(0)
    step = pl.program_id(0)

    @pl.when(step == 0)
    def _():
        copies = []
        for n in range(count):
            at = 0
            for m, piece in enumerate(pieces[n]):
                target = rows[n].at[:, pl.ds(at, piece.shape[1]), :]
                copies.append(pltpu.make_async_copy(piece, target, sems.at[2 * n + m]))
                at += piece.shape[1]
        for copy in copies:
            copy.start()
        for copy in copies:
            copy.wait()

    def total(which):
        value = acc_in[step, which] if last else None
        for n in range(count):
            weight = down[n][...] if which == 2 else gate_up[n][which]
            part = lax.dot_general(
                rows[n][1 if which == 2 else 0], weight, NT, preferred_element_type=jnp.float32
            )
            value = part if value is None else value + part
        return value

    if not last:
        for which in range(3):
            acc_out[step, which] = total(which)
        return
    ut_ref = refs.pop(0)

    @pl.when(step == 0)
    def _():
        ut_ref[...] = jnp.zeros_like(ut_ref)

    sides = activations(total(0), total(1), total(2))
    for n, side in enumerate(sides):
        ut_ref[pl.ds(n * K, K), :] += lax.dot_general(
            proj_ref[pl.ds(n * K, K), :], side, NT, preferred_element_type=jnp.float32
        )

    @pl.when(step == pl.num_programs(0) - 1)
    def _():
        half = mine_ref.shape[0]
        core = lax.rem(where_ref[0], 2)
        mine_ref[...] = ut_ref[pl.ds(pl.multiple_of(core * half, 8), half), :]
        theirs_ref[...] = ut_ref[pl.ds(pl.multiple_of((1 - core) * half, 8), half), :]


def matmul_step(where, blocks, w_gate_up, w_down, acc=None, unit_proj_t=None):
    last = acc is not None
    count = len(blocks)
    unit_width = w_down.shape[0]
    width = blocks[0][1][0].shape[2]
    tokens = sum(piece.shape[1] for piece in blocks[0][1])
    tile = 256
    tiles = unit_width // tile
    whole = pl.BlockSpec(memory_space=pltpu.VMEM)

    in_specs, operands = [], []
    for _, pieces in blocks:
        for piece in pieces:
            in_specs.append(pl.BlockSpec(memory_space=pl.ANY))
            operands.append(piece)
    for owner, _ in blocks:
        in_specs.append(pl.BlockSpec((2, tile, width), lambda i, r, o=owner: (0, i, r[o])))
        operands.append(pltpu.with_memory_space_constraint(w_gate_up, pltpu.HBM))
    for owner, _ in blocks:
        in_specs.append(pl.BlockSpec((tile, width), lambda i, r, o=owner: (i, r[o])))
        operands.append(pltpu.with_memory_space_constraint(w_down, pltpu.HBM))
    need = count * width * (2 * tokens + 2 * 3 * tile) * 2 + 6 * MIB
    scratch = [pltpu.VMEM((2, tokens, width), jnp.bfloat16) for _ in blocks]
    scratch.append(pltpu.SemaphoreType.DMA((2 * count,)))
    if last:
        in_specs.append(whole)
        operands.append(pltpu.with_memory_space_constraint(acc, pltpu.VMEM))
        in_specs.append(pl.BlockSpec((3 * K, tile), lambda i, r: (0, i)))
        operands.append(unit_proj_t)
        half = jax.ShapeDtypeStruct((3 * K // 2, tokens), jnp.float32)
        out_shape = (half, half)
        out_specs = (pl.BlockSpec(half.shape, lambda i, r: (0, 0)),) * 2
        scratch.append(pltpu.VMEM((3 * K, tokens), jnp.float32))
        need += 6 * MIB
    else:
        out_shape = pltpu.VMEM((tiles, 3, tokens, tile), jnp.float32)
        out_specs = whole
    return pl.pallas_call(
        functools.partial(matmul_kernel, count, last),
        out_shape=out_shape,
        grid_spec=pltpu.PrefetchScalarGridSpec(
            num_scalar_prefetch=1,
            grid=(tiles,),
            in_specs=in_specs,
            out_specs=out_specs,
            scratch_shapes=scratch,
        ),
        compiler_params=pltpu.CompilerParams(vmem_limit_bytes=need),
        cost_estimate=pl.CostEstimate(
            flops=2 * tokens * 3 * unit_width * width * count,
            bytes_accessed=3 * unit_width * width * count * 2,
            transcendentals=0,
        ),
        name="matmul",
    )(where, *operands)


def sketch_kernel(where_ref, feat_ref, mine_ref, other_ref, out_ref, unit_ref):
    half = mine_ref.shape[0]
    core = lax.rem(where_ref[0], 2)
    unit_ref[pl.ds(pl.multiple_of(core * half, 8), half), :] = mine_ref[...]
    unit_ref[pl.ds(pl.multiple_of((1 - core) * half, 8), half), :] = other_ref[...]
    for w in range(3):
        in_ref, side_ref = (feat_ref, unit_ref) if w < 2 else (unit_ref, feat_ref)
        right = side_ref[pl.ds(w * K, K), :]
        parts = [
            lax.dot_general(
                in_ref[pl.ds(w * K + odd, K // 2, stride=2), :],
                right,
                NT,
                precision=lax.Precision.HIGHEST,
                preferred_element_type=jnp.float32,
            )
            for odd in range(2)
        ]
        out_ref[w] = jnp.concatenate(parts, axis=1) * SEQ ** (-0.5)


def sketch_own(where, feat_t, mine, other):
    whole = pl.BlockSpec(memory_space=pltpu.VMEM)
    return pl.pallas_call(
        sketch_kernel,
        out_shape=jax.ShapeDtypeStruct((3, K // 2, 2 * K), jnp.float32),
        in_specs=[pl.BlockSpec(memory_space=pltpu.SMEM), whole, whole, whole],
        out_specs=whole,
        scratch_shapes=[pltpu.VMEM((3 * K, SEQ), jnp.float32)],
        name="sketch",
    )(where, feat_t, mine, other)


def precond_kernel(row_ref, p_ref, *refs):
    sketches, out_ref, sums = refs[:ROWS], refs[ROWS], refs[ROWS + 1]
    height = p_ref.shape[1]
    lanes = 2 * K
    group = 32
    ones = jnp.ones((8, lanes), jnp.float32)

    @pl.loop(0, height // group)
    def _(g):
        at = pl.ds(pl.multiple_of(g * group, group), group)
        totals = [jnp.zeros((group, lanes), jnp.float32) for _ in range(ROWS)]
        for q in range(K // 2):
            part = p_ref[0, at, pl.ds(q * lanes, lanes)]
            for n in range(ROWS):
                totals[n] = totals[n] + part * sketches[n][0, pl.ds(q, 1), :]
        for n in range(ROWS):
            sums[n, at, :] = totals[n]

    for n in range(ROWS):
        seq = row_ref[0] ^ n
        line = lax.dot_general(
            ones,
            sums[n],
            NT,
            precision=lax.Precision.HIGHEST,
            preferred_element_type=jnp.float32,
        )
        out_ref[0, pl.ds(seq, 1), :] = line[:1]


def apply_precond(row, precond, sketches):
    height, order = precond.shape[1:]
    piece = pl.BlockSpec((1, K // 2, 2 * K), lambda w, r: (w, 0, 0))
    return pl.pallas_call(
        precond_kernel,
        out_shape=jax.ShapeDtypeStruct((3, ROWS, height), jnp.float32),
        grid_spec=pltpu.PrefetchScalarGridSpec(
            num_scalar_prefetch=1,
            grid=(3,),
            in_specs=[pl.BlockSpec((1, height, order), lambda w, r: (w, 0, 0))] + [piece] * ROWS,
            out_specs=pl.BlockSpec((1, ROWS, height), lambda w, r: (w, 0, 0)),
            scratch_shapes=[pltpu.VMEM((ROWS, height, 2 * K), jnp.float32)],
        ),
        compiler_params=pltpu.CompilerParams(vmem_limit_bytes=24 * MIB),
        name="precond",
    )(row, precond, *sketches)


A, C, Y, D = range(4)
INNER = [(t * ROWS + a, t * ROWS + b) for t in range(TENSOR) for a, b in ((1, 2), (2, 1))]
OUTER = [(t * ROWS + a, t * ROWS + b) for t in range(TENSOR) for a, b in ((1, 0), (2, 3))]


def other_core(value):
    return send(value, swap_with(1))


def other_chip(value):
    return send(value, swap_with(2))


def tie(*values):
    return lax.optimization_barrier(values)


def local_split(hidden_in, out_grad, w_gate_up, w_down, feat_proj, unit_proj, precond):
    tensor, row = lax.axis_index("tensor"), lax.axis_index("dp")
    inner = jnp.logical_or(row == 1, row == 2)
    where = jnp.stack([tensor, tensor ^ 1, tensor ^ 2, tensor ^ 3]).astype(jnp.int32)
    step = functools.partial(matmul_step, where)

    own = jnp.stack([hidden_in, out_grad])
    near = send(own, swap_rows(1))
    middle = send(own, INNER)
    own_y = other_chip(own)
    own_c = other_core(own)
    feat_t = jnp.concatenate(
        [
            lax.dot_general(
                feat_proj[:, : 2 * K], hidden_in, (((0,), (1,)), ((), ())), preferred_element_type=jnp.float32
            ),
            lax.dot_general(
                feat_proj[:, 2 * K :], out_grad, (((0,), (1,)), ((), ())), preferred_element_type=jnp.float32
            ),
        ],
        axis=0,
    )
    feat_t = feat_t + other_core(feat_t)
    unit_proj_t = unit_proj.T
    near, middle, own_y, own_c, unit_proj_t, feat_t = tie(near, middle, own_y, own_c, unit_proj_t, feat_t)

    near_c = other_core(near)
    passed = send(middle, OUTER)
    middle_2 = send(near, INNER)
    near_y = other_chip(near)
    own_d = other_core(own_y)
    feat_y = other_chip(feat_t)
    acc = step([(A, (own, near)), (C, (own_c, near_c))], w_gate_up, w_down)
    passed, middle_2, near_y, own_d, feat_y, acc = tie(passed, middle_2, near_y, own_d, feat_y, acc)
    feat_t = feat_t + feat_y

    near_d = other_core(near_y)
    third = jnp.where(inner, middle, passed)
    passed_2 = send(middle_2, OUTER)
    third_y = other_chip(third)
    third_c = other_core(third)
    mine_0, theirs_0 = step(
        [(Y, (own_y, near_y)), (D, (own_d, near_d))], w_gate_up, w_down, acc, unit_proj_t
    )
    passed_2, third_y, third_c, mine_0, theirs_0 = tie(passed_2, third_y, third_c, mine_0, theirs_0)

    fourth = jnp.where(inner, middle_2, passed_2)
    fourth_c = other_core(fourth)
    fourth_y = other_chip(fourth)
    third_d = other_core(third_y)
    mine_0 = mine_0 + other_core(theirs_0)
    acc = step([(A, (third, fourth)), (C, (third_c, fourth_c))], w_gate_up, w_down)
    fourth_y, third_d, mine_0, acc = tie(fourth_y, third_d, mine_0, acc)

    fourth_d = other_core(fourth_y)
    mine_1, theirs_1 = step(
        [(Y, (third_y, fourth_y)), (D, (third_d, fourth_d))], w_gate_up, w_down, acc, unit_proj_t
    )

    part = mine_0[:, :SEQ] + send(mine_0[:, SEQ:], swap_rows(1))
    mine_1 = mine_1 + other_core(theirs_1)
    low, high = mine_1[:, :SEQ], mine_1[:, SEQ:]
    part = part + send(jnp.where(inner, high, low), swap_rows(2)) + send(jnp.where(inner, low, high), swap_rows(3))
    part = part + other_chip(part)
    other = other_core(part)
    sketch = sketch_own(where, feat_t, part, other)
    sketches = [sketch] + [send(sketch, swap_rows(n)) for n in range(1, ROWS)]
    return apply_precond(row.astype(jnp.int32).reshape(1), precond, sketches)


def local(hidden_in, out_grad, w_gate_up, w_down, feat_proj, unit_proj, precond):
    fits = (
        lax.axis_size("tensor") == TENSOR
        and lax.axis_size("dp") == ROWS
        and hidden_in.shape[0] == SEQ
        and w_down.shape[0] % 256 == 0
    )
    step = local_split if fits else local_plain
    return step(hidden_in, out_grad, w_gate_up, w_down, feat_proj, unit_proj, precond)


def solution(mesh):
    in_specs = (
        P(("groups", "dp"), "tensor"),
        P(("groups", "dp"), "tensor"),
        P(None, ("tensor", "dp"), None),
        P(("tensor", "dp"), None),
        P("tensor", None),
        P(("tensor", "dp"), None),
        P(None, ("tensor", "dp"), None),
    )
    out_specs = P(None, "groups", ("tensor", "dp"))
    return jax.shard_map(local, mesh=mesh, in_specs=in_specs, out_specs=out_specs, check_vma=False)
```

```python
import functools

import jax
import jax.numpy as jnp
from jax import lax
from jax.experimental import pallas as pl
from jax.experimental.pallas import tpu as pltpu
from jax.sharding import PartitionSpec as P

K = 64
SEQ = 128
BOTH = ("tensor", "dp")
NT = (((1,), (1,)), ((), ()))
MIB = 1 << 20


def project_pair(rows_in, rows_out, columns):
    return jnp.concatenate(
        [
            jnp.dot(rows_in, columns[:, : 2 * K], preferred_element_type=jnp.float32),
            jnp.dot(rows_out, columns[:, 2 * K :], preferred_element_type=jnp.float32),
        ],
        axis=1,
    )


def form_sketch(in_side, out_side):
    seq_count = in_side.shape[0] // SEQ
    left_rows = in_side.reshape(seq_count, SEQ, 3, K)
    right_rows = out_side.reshape(seq_count, SEQ, 3, K)
    sketch = jnp.einsum("stwi,stwj->wsij", left_rows, right_rows, precision=lax.Precision.HIGHEST)
    sketch = sketch * SEQ ** (-0.5)
    return sketch.reshape(3, seq_count, K * K)


def activations(gate_pre, up_pre, hid_grad):
    gate_sig = jax.nn.sigmoid(gate_pre)
    silu_gate = gate_pre * gate_sig
    hidden = (silu_gate * up_pre).astype(jnp.bfloat16)
    gate_grad = (hid_grad * up_pre * gate_sig * (1.0 + gate_pre * (1.0 - gate_sig))).astype(
        jnp.bfloat16
    )
    up_grad = (hid_grad * silu_gate).astype(jnp.bfloat16)
    return gate_grad, up_grad, hidden


def local_plain(hidden_in, out_grad, w_gate_up, w_down, feat_proj, unit_proj, precond):
    unit_width, model_width = w_down.shape
    w_both = w_gate_up.reshape(2 * unit_width, model_width)
    paired = jnp.stack([hidden_in, out_grad])
    columns = lax.all_gather(feat_proj, "tensor", axis=0, tiled=True)
    rows_all = lax.all_gather(paired, "dp", axis=1, tiled=True)
    pieces = lax.all_gather(rows_all, "tensor", axis=2, tiled=True)
    pre_act = lax.dot_general(pieces[0], w_both, NT, preferred_element_type=jnp.float32)
    hid_grad = lax.dot_general(pieces[1], w_down, NT, preferred_element_type=jnp.float32)
    feat_side = project_pair(pieces[0], pieces[1], columns)
    sides = activations(pre_act[:, :unit_width], pre_act[:, unit_width:], hid_grad)
    unit_part = jnp.concatenate(
        [
            jnp.dot(side, unit_proj[:, n * K : (n + 1) * K], preferred_element_type=jnp.float32)
            for n, side in enumerate(sides)
        ],
        axis=1,
    )
    unit_side = lax.psum(unit_part, BOTH)
    in_side = jnp.concatenate([feat_side[:, : 2 * K], unit_side[:, 2 * K :]], axis=1)
    out_side = jnp.concatenate([unit_side[:, : 2 * K], feat_side[:, 2 * K :]], axis=1)
    sketch = form_sketch(in_side, out_side)
    return jnp.einsum("wrc,wsc->wsr", precond, sketch, precision=lax.Precision.HIGHEST)


TENSOR = 4
ROWS = 4


def swap_with(flip):
    return [(t * ROWS + z, (t ^ flip) * ROWS + z) for t in range(TENSOR) for z in range(ROWS)]


def swap_rows(flip):
    return [(t * ROWS + z, t * ROWS + (z ^ flip)) for t in range(TENSOR) for z in range(ROWS)]


def send(value, pairs):
    return lax.ppermute(value, BOTH, pairs)


def matmul_kernel(count, last, *refs):
    refs = list(refs)
    where_ref = refs.pop(0)
    pieces = [(refs.pop(0), refs.pop(0)) for _ in range(count)]
    gate_up = [refs.pop(0) for _ in range(count)]
    down = [refs.pop(0) for _ in range(count)]
    if last:
        acc_in, proj_ref, mine_ref, theirs_ref = (refs.pop(0) for _ in range(4))
    else:
        acc_out = refs.pop(0)
    rows = [refs.pop(0) for _ in range(count)]
    sems = refs.pop(0)
    step = pl.program_id(0)

    @pl.when(step == 0)
    def _():
        copies = []
        for n in range(count):
            at = 0
            for m, piece in enumerate(pieces[n]):
                target = rows[n].at[:, pl.ds(at, piece.shape[1]), :]
                copies.append(pltpu.make_async_copy(piece, target, sems.at[2 * n + m]))
                at += piece.shape[1]
        for copy in copies:
            copy.start()
        for copy in copies:
            copy.wait()

    def total(which):
        value = acc_in[step, which] if last else None
        for n in range(count):
            weight = down[n][...] if which == 2 else gate_up[n][which]
            part = lax.dot_general(
                rows[n][1 if which == 2 else 0], weight, NT, preferred_element_type=jnp.float32
            )
            value = part if value is None else value + part
        return value

    if not last:
        for which in range(3):
            acc_out[step, which] = total(which)
        return
    ut_ref = refs.pop(0)

    @pl.when(step == 0)
    def _():
        ut_ref[...] = jnp.zeros_like(ut_ref)

    sides = activations(total(0), total(1), total(2))
    for n, side in enumerate(sides):
        ut_ref[pl.ds(n * K, K), :] += lax.dot_general(
            proj_ref[pl.ds(n * K, K), :], side, NT, preferred_element_type=jnp.float32
        )

    @pl.when(step == pl.num_programs(0) - 1)
    def _():
        half = mine_ref.shape[0]
        core = lax.rem(where_ref[0], 2)
        mine_ref[...] = ut_ref[pl.ds(pl.multiple_of(core * half, 8), half), :]
        theirs_ref[...] = ut_ref[pl.ds(pl.multiple_of((1 - core) * half, 8), half), :]


def matmul_step(where, blocks, w_gate_up, w_down, acc=None, unit_proj_t=None):
    last = acc is not None
    count = len(blocks)
    unit_width = w_down.shape[0]
    width = blocks[0][1][0].shape[2]
    tokens = sum(piece.shape[1] for piece in blocks[0][1])
    tile = 256
    tiles = unit_width // tile
    whole = pl.BlockSpec(memory_space=pltpu.VMEM)

    in_specs, operands = [], []
    for _, pieces in blocks:
        for piece in pieces:
            in_specs.append(whole)
            operands.append(pltpu.with_memory_space_constraint(piece, pltpu.VMEM))
    for owner, _ in blocks:
        in_specs.append(pl.BlockSpec((2, tile, width), lambda i, r, o=owner: (0, i, r[o])))
        operands.append(pltpu.with_memory_space_constraint(w_gate_up, pltpu.HBM))
    for owner, _ in blocks:
        in_specs.append(pl.BlockSpec((tile, width), lambda i, r, o=owner: (i, r[o])))
        operands.append(pltpu.with_memory_space_constraint(w_down, pltpu.HBM))
    need = count * width * (2 * tokens + 2 * 3 * tile) * 2 + 4 * MIB
    scratch = [pltpu.VMEM((2, tokens, width), jnp.bfloat16) for _ in blocks]
    scratch.append(pltpu.SemaphoreType.DMA((2 * count,)))
    if last:
        in_specs.append(whole)
        operands.append(pltpu.with_memory_space_constraint(acc, pltpu.VMEM))
        out_shape, out_specs = [], []
    else:
        out_shape, out_specs = [pltpu.VMEM((tiles, 3, tokens, tile), jnp.float32)], [whole]
    if last:
        in_specs.append(pl.BlockSpec((3 * K, tile), lambda i, r: (0, i)))
        operands.append(unit_proj_t)
        half = jax.ShapeDtypeStruct((3 * K // 2, tokens), jnp.float32)
        out_shape += [half] * 2
        out_specs += [pl.BlockSpec(half.shape, lambda i, r: (0, 0))] * 2
        scratch.append(pltpu.VMEM((3 * K, tokens), jnp.float32))
        need += 4 * MIB
    return pl.pallas_call(
        functools.partial(matmul_kernel, count, last),
        out_shape=out_shape,
        grid_spec=pltpu.PrefetchScalarGridSpec(
            num_scalar_prefetch=1,
            grid=(tiles,),
            in_specs=in_specs,
            out_specs=out_specs,
            scratch_shapes=scratch,
        ),
        compiler_params=pltpu.CompilerParams(vmem_limit_bytes=need),
        cost_estimate=pl.CostEstimate(
            flops=2 * tokens * 3 * unit_width * width * count,
            bytes_accessed=3 * unit_width * width * count * 2,
            transcendentals=0,
        ),
        name="matmul",
    )(where, *operands)


def sketch_kernel(where_ref, feat_ref, mine_ref, other_ref, out_ref, unit_ref):
    half = mine_ref.shape[0]
    core = lax.rem(where_ref[0], 2)
    unit_ref[pl.ds(pl.multiple_of(core * half, 8), half), :] = mine_ref[...]
    unit_ref[pl.ds(pl.multiple_of((1 - core) * half, 8), half), :] = other_ref[...]
    for w in range(3):
        in_ref, side_ref = (feat_ref, unit_ref) if w < 2 else (unit_ref, feat_ref)
        right = side_ref[pl.ds(w * K, K), :]
        parts = [
            lax.dot_general(
                in_ref[pl.ds(w * K + odd, K // 2, stride=2), :],
                right,
                NT,
                precision=lax.Precision.HIGHEST,
                preferred_element_type=jnp.float32,
            )
            for odd in range(2)
        ]
        out_ref[w] = jnp.concatenate(parts, axis=1) * SEQ ** (-0.5)


def sketch_own(where, feat_t, mine, other):
    whole = pl.BlockSpec(memory_space=pltpu.VMEM)
    return pl.pallas_call(
        sketch_kernel,
        out_shape=jax.ShapeDtypeStruct((3, K // 2, 2 * K), jnp.float32),
        in_specs=[pl.BlockSpec(memory_space=pltpu.SMEM), whole, whole, whole],
        out_specs=whole,
        scratch_shapes=[pltpu.VMEM((3 * K, SEQ), jnp.float32)],
        compiler_params=pltpu.CompilerParams(vmem_limit_bytes=4 * MIB),
        name="sketch",
    )(where, feat_t, mine, other)


def precond_kernel(row_ref, p_ref, *refs):
    sketches, out_ref, sums = refs[:ROWS], refs[ROWS], refs[ROWS + 1]
    height = p_ref.shape[1]
    lanes = 2 * K
    group = 32
    ones = jnp.ones((8, lanes), jnp.float32)

    @pl.loop(0, height // group)
    def _(g):
        at = pl.ds(pl.multiple_of(g * group, group), group)
        totals = [jnp.zeros((group, lanes), jnp.float32) for _ in range(ROWS)]
        for q in range(K // 2):
            part = p_ref[0, at, pl.ds(q * lanes, lanes)]
            for n in range(ROWS):
                totals[n] = totals[n] + part * sketches[n][0, pl.ds(q, 1), :]
        for n in range(ROWS):
            sums[n, at, :] = totals[n]

    for n in range(ROWS):
        seq = row_ref[0] ^ n
        line = lax.dot_general(
            ones,
            sums[n],
            NT,
            precision=lax.Precision.HIGHEST,
            preferred_element_type=jnp.float32,
        )
        out_ref[0, pl.ds(seq, 1), :] = line[:1]


def apply_precond(row, precond, sketches):
    height, order = precond.shape[1:]
    piece = pl.BlockSpec((1, K // 2, 2 * K), lambda w, r: (w, 0, 0))
    return pl.pallas_call(
        precond_kernel,
        out_shape=jax.ShapeDtypeStruct((3, ROWS, height), jnp.float32),
        grid_spec=pltpu.PrefetchScalarGridSpec(
            num_scalar_prefetch=1,
            grid=(3,),
            in_specs=[pl.BlockSpec((1, height, order), lambda w, r: (w, 0, 0))] + [piece] * ROWS,
            out_specs=pl.BlockSpec((1, ROWS, height), lambda w, r: (w, 0, 0)),
            scratch_shapes=[pltpu.VMEM((ROWS, height, 2 * K), jnp.float32)],
        ),
        compiler_params=pltpu.CompilerParams(vmem_limit_bytes=12 * MIB),
        name="precond",
    )(row, precond, *sketches)


A, C, Y, D = range(4)
INNER = [(t * ROWS + a, t * ROWS + b) for t in range(TENSOR) for a, b in ((1, 2), (2, 1))]
OUTER = [(t * ROWS + a, t * ROWS + b) for t in range(TENSOR) for a, b in ((1, 0), (2, 3))]


def other_core(value):
    return send(value, swap_with(1))


def other_chip(value):
    return send(value, swap_with(2))


def tie(*values):
    return lax.optimization_barrier(values)


def local_split(hidden_in, out_grad, w_gate_up, w_down, feat_proj, unit_proj, precond):
    tensor, row = lax.axis_index("tensor"), lax.axis_index("dp")
    inner = jnp.logical_or(row == 1, row == 2)
    where = jnp.stack([tensor, tensor ^ 1, tensor ^ 2, tensor ^ 3]).astype(jnp.int32)
    row = row.astype(jnp.int32).reshape(1)
    hidden_in, out_grad, where, row, inner = tie(hidden_in, out_grad, where, row, inner)
    step = functools.partial(matmul_step, where)

    own = jnp.stack([hidden_in, out_grad])
    near = send(own, swap_rows(1))
    middle = send(own, INNER)
    own_y = other_chip(own)
    own_c = other_core(own)
    feat_t = jnp.concatenate(
        [
            lax.dot_general(
                feat_proj[:, : 2 * K], hidden_in, (((0,), (1,)), ((), ())), preferred_element_type=jnp.float32
            ),
            lax.dot_general(
                feat_proj[:, 2 * K :], out_grad, (((0,), (1,)), ((), ())), preferred_element_type=jnp.float32
            ),
        ],
        axis=0,
    )
    feat_t = feat_t + other_core(feat_t)
    unit_proj_t = unit_proj.T
    near, middle, own_y, own_c, unit_proj_t, feat_t = tie(near, middle, own_y, own_c, unit_proj_t, feat_t)

    near_c = other_core(near)
    passed = send(middle, OUTER)
    middle_2 = send(near, INNER)
    near_y = other_chip(near)
    own_d = other_core(own_y)
    feat_y = other_chip(feat_t)
    (acc,) = step([(A, (own, near)), (C, (own_c, near_c))], w_gate_up, w_down)
    passed, middle_2, near_y, own_d, feat_y, acc = tie(passed, middle_2, near_y, own_d, feat_y, acc)
    feat_t = feat_t + feat_y

    near_d = other_core(near_y)
    third = jnp.where(inner, middle, passed)
    passed_2 = send(middle_2, OUTER)
    third_y = other_chip(third)
    third_c = other_core(third)
    mine_0, theirs_0 = step(
        [(Y, (own_y, near_y)), (D, (own_d, near_d))], w_gate_up, w_down, acc, unit_proj_t
    )
    passed_2, third_y, third_c, mine_0, theirs_0, feat_t = tie(
        passed_2, third_y, third_c, mine_0, theirs_0, feat_t
    )

    fourth = jnp.where(inner, middle_2, passed_2)
    fourth_c = other_core(fourth)
    fourth_y = other_chip(fourth)
    third_d = other_core(third_y)
    mine_0 = mine_0 + other_core(theirs_0)
    part = mine_0[:, :SEQ] + send(mine_0[:, SEQ:], swap_rows(1))
    (acc,) = step([(A, (third, fourth)), (C, (third_c, fourth_c))], w_gate_up, w_down)
    fourth_y, third_d, part, acc = tie(fourth_y, third_d, part, acc)

    fourth_d = other_core(fourth_y)
    mine_1, theirs_1 = step(
        [(Y, (third_y, fourth_y)), (D, (third_d, fourth_d))], w_gate_up, w_down, acc, unit_proj_t
    )

    mine_1 = mine_1 + other_core(theirs_1)
    low, high = mine_1[:, :SEQ], mine_1[:, SEQ:]
    part = part + send(jnp.where(inner, high, low), swap_rows(2)) + send(jnp.where(inner, low, high), swap_rows(3))
    part = part + other_chip(part)
    other = other_core(part)
    sketch = sketch_own(where, feat_t, part, other)
    sketches = [sketch] + [send(sketch, swap_rows(n)) for n in range(1, ROWS)]
    return apply_precond(row, precond, sketches)


def local(hidden_in, out_grad, w_gate_up, w_down, feat_proj, unit_proj, precond):
    fits = (
        lax.axis_size("tensor") == TENSOR
        and lax.axis_size("dp") == ROWS
        and hidden_in.shape[0] == SEQ
        and w_down.shape[0] % 256 == 0
    )
    step = local_split if fits else local_plain
    return step(hidden_in, out_grad, w_gate_up, w_down, feat_proj, unit_proj, precond)


def solution(mesh):
    in_specs = (
        P(("groups", "dp"), "tensor"),
        P(("groups", "dp"), "tensor"),
        P(None, ("tensor", "dp"), None),
        P(("tensor", "dp"), None),
        P("tensor", None),
        P(("tensor", "dp"), None),
        P(None, ("tensor", "dp"), None),
    )
    out_specs = P(None, "groups", ("tensor", "dp"))
    return jax.shard_map(local, mesh=mesh, in_specs=in_specs, out_specs=out_specs, check_vma=False)
```

```python
import functools

import jax
import jax.numpy as jnp
from jax import lax
from jax.experimental import pallas as pl
from jax.experimental.pallas import tpu as pltpu
from jax.sharding import PartitionSpec as P

K = 64
SEQ = 128
BOTH = ("tensor", "dp")
NT = (((1,), (1,)), ((), ()))
MIB = 1 << 20


def project_pair(rows_in, rows_out, columns):
    return jnp.concatenate(
        [
            jnp.dot(rows_in, columns[:, : 2 * K], preferred_element_type=jnp.float32),
            jnp.dot(rows_out, columns[:, 2 * K :], preferred_element_type=jnp.float32),
        ],
        axis=1,
    )


def form_sketch(in_side, out_side):
    seq_count = in_side.shape[0] // SEQ
    left_rows = in_side.reshape(seq_count, SEQ, 3, K)
    right_rows = out_side.reshape(seq_count, SEQ, 3, K)
    sketch = jnp.einsum("stwi,stwj->wsij", left_rows, right_rows, precision=lax.Precision.HIGHEST)
    sketch = sketch * SEQ ** (-0.5)
    return sketch.reshape(3, seq_count, K * K)


def activations(gate_pre, up_pre, hid_grad):
    gate_sig = jax.nn.sigmoid(gate_pre)
    silu_gate = gate_pre * gate_sig
    hidden = (silu_gate * up_pre).astype(jnp.bfloat16)
    gate_grad = (hid_grad * up_pre * gate_sig * (1.0 + gate_pre * (1.0 - gate_sig))).astype(
        jnp.bfloat16
    )
    up_grad = (hid_grad * silu_gate).astype(jnp.bfloat16)
    return gate_grad, up_grad, hidden


def local_plain(hidden_in, out_grad, w_gate_up, w_down, feat_proj, unit_proj, precond):
    unit_width, model_width = w_down.shape
    w_both = w_gate_up.reshape(2 * unit_width, model_width)
    paired = jnp.stack([hidden_in, out_grad])
    columns = lax.all_gather(feat_proj, "tensor", axis=0, tiled=True)
    rows_all = lax.all_gather(paired, "dp", axis=1, tiled=True)
    pieces = lax.all_gather(rows_all, "tensor", axis=2, tiled=True)
    pre_act = lax.dot_general(pieces[0], w_both, NT, preferred_element_type=jnp.float32)
    hid_grad = lax.dot_general(pieces[1], w_down, NT, preferred_element_type=jnp.float32)
    feat_side = project_pair(pieces[0], pieces[1], columns)
    sides = activations(pre_act[:, :unit_width], pre_act[:, unit_width:], hid_grad)
    unit_part = jnp.concatenate(
        [
            jnp.dot(side, unit_proj[:, n * K : (n + 1) * K], preferred_element_type=jnp.float32)
            for n, side in enumerate(sides)
        ],
        axis=1,
    )
    unit_side = lax.psum(unit_part, BOTH)
    in_side = jnp.concatenate([feat_side[:, : 2 * K], unit_side[:, 2 * K :]], axis=1)
    out_side = jnp.concatenate([unit_side[:, : 2 * K], feat_side[:, 2 * K :]], axis=1)
    sketch = form_sketch(in_side, out_side)
    return jnp.einsum("wrc,wsc->wsr", precond, sketch, precision=lax.Precision.HIGHEST)


TENSOR = 4
ROWS = 4


def swap_with(flip):
    return [(t * ROWS + z, (t ^ flip) * ROWS + z) for t in range(TENSOR) for z in range(ROWS)]


def swap_rows(flip):
    return [(t * ROWS + z, t * ROWS + (z ^ flip)) for t in range(TENSOR) for z in range(ROWS)]


def send(value, pairs):
    return lax.ppermute(value, BOTH, pairs)


def matmul_kernel(count, last, *refs):
    refs = list(refs)
    where_ref = refs.pop(0)
    pieces = [(refs.pop(0), refs.pop(0)) for _ in range(count)]
    gate_up = [refs.pop(0) for _ in range(count)]
    down = [refs.pop(0) for _ in range(count)]
    if last:
        acc_in, proj_ref, mine_ref, theirs_ref = (refs.pop(0) for _ in range(4))
    else:
        acc_out = refs.pop(0)
    rows = [refs.pop(0) for _ in range(count)]
    sems = refs.pop(0)
    step = pl.program_id(0)

    @pl.when(step == 0)
    def _():
        copies = []
        for n in range(count):
            at = 0
            for m, piece in enumerate(pieces[n]):
                target = rows[n].at[:, pl.ds(at, piece.shape[1]), :]
                copies.append(pltpu.make_async_copy(piece, target, sems.at[2 * n + m]))
                at += piece.shape[1]
        for copy in copies:
            copy.start()
        for copy in copies:
            copy.wait()

    def total(which):
        value = acc_in[step, which] if last else None
        for n in range(count):
            weight = down[n][...] if which == 2 else gate_up[n][which]
            part = lax.dot_general(
                rows[n][1 if which == 2 else 0], weight, NT, preferred_element_type=jnp.float32
            )
            value = part if value is None else value + part
        return value

    if not last:
        for which in range(3):
            acc_out[step, which] = total(which)
        return
    ut_ref = refs.pop(0)

    @pl.when(step == 0)
    def _():
        ut_ref[...] = jnp.zeros_like(ut_ref)

    sides = activations(total(0), total(1), total(2))
    for n, side in enumerate(sides):
        ut_ref[pl.ds(n * K, K), :] += lax.dot_general(
            proj_ref[pl.ds(n * K, K), :], side, NT, preferred_element_type=jnp.float32
        )

    @pl.when(step == pl.num_programs(0) - 1)
    def _():
        half = mine_ref.shape[0]
        core = lax.rem(where_ref[0], 2)
        mine_ref[...] = ut_ref[pl.ds(pl.multiple_of(core * half, 8), half), :]
        theirs_ref[...] = ut_ref[pl.ds(pl.multiple_of((1 - core) * half, 8), half), :]


def matmul_step(where, blocks, w_gate_up, w_down, acc=None, unit_proj_t=None):
    last = acc is not None
    count = len(blocks)
    unit_width = w_down.shape[0]
    width = blocks[0][1][0].shape[2]
    tokens = sum(piece.shape[1] for piece in blocks[0][1])
    tile = 256
    tiles = unit_width // tile
    whole = pl.BlockSpec(memory_space=pltpu.VMEM)

    in_specs, operands = [], []
    for _, pieces in blocks:
        for piece in pieces:
            in_specs.append(whole)
            operands.append(pltpu.with_memory_space_constraint(piece, pltpu.VMEM))
    for owner, _ in blocks:
        in_specs.append(pl.BlockSpec((2, tile, width), lambda i, r, o=owner: (0, i, r[o])))
        operands.append(pltpu.with_memory_space_constraint(w_gate_up, pltpu.HBM))
    for owner, _ in blocks:
        in_specs.append(pl.BlockSpec((tile, width), lambda i, r, o=owner: (i, r[o])))
        operands.append(pltpu.with_memory_space_constraint(w_down, pltpu.HBM))
    need = count * width * (2 * tokens + 2 * 3 * tile) * 2 + 4 * MIB
    scratch = [pltpu.VMEM((2, tokens, width), jnp.bfloat16) for _ in blocks]
    scratch.append(pltpu.SemaphoreType.DMA((2 * count,)))
    if last:
        in_specs.append(whole)
        operands.append(pltpu.with_memory_space_constraint(acc, pltpu.VMEM))
        out_shape, out_specs = [], []
    else:
        out_shape, out_specs = [pltpu.VMEM((tiles, 3, tokens, tile), jnp.float32)], [whole]
    if last:
        in_specs.append(pl.BlockSpec((3 * K, tile), lambda i, r: (0, i)))
        operands.append(unit_proj_t)
        half = jax.ShapeDtypeStruct((3 * K // 2, tokens), jnp.float32)
        out_shape += [half] * 2
        out_specs += [pl.BlockSpec(half.shape, lambda i, r: (0, 0))] * 2
        scratch.append(pltpu.VMEM((3 * K, tokens), jnp.float32))
        need += 4 * MIB
    return pl.pallas_call(
        functools.partial(matmul_kernel, count, last),
        out_shape=out_shape,
        grid_spec=pltpu.PrefetchScalarGridSpec(
            num_scalar_prefetch=1,
            grid=(tiles,),
            in_specs=in_specs,
            out_specs=out_specs,
            scratch_shapes=scratch,
        ),
        compiler_params=pltpu.CompilerParams(vmem_limit_bytes=need),
        cost_estimate=pl.CostEstimate(
            flops=2 * tokens * 3 * unit_width * width * count,
            bytes_accessed=3 * unit_width * width * count * 2,
            transcendentals=0,
        ),
        name="matmul",
    )(where, *operands)


def sketch_kernel(where_ref, feat_ref, mine_ref, other_ref, out_ref, unit_ref):
    half = mine_ref.shape[0]
    core = lax.rem(where_ref[0], 2)
    unit_ref[pl.ds(pl.multiple_of(core * half, 8), half), :] = mine_ref[...]
    unit_ref[pl.ds(pl.multiple_of((1 - core) * half, 8), half), :] = other_ref[...]
    for w in range(3):
        in_ref, side_ref = (feat_ref, unit_ref) if w < 2 else (unit_ref, feat_ref)
        right = side_ref[pl.ds(w * K, K), :]
        parts = [
            lax.dot_general(
                in_ref[pl.ds(w * K + odd, K // 2, stride=2), :],
                right,
                NT,
                precision=lax.Precision.HIGHEST,
                preferred_element_type=jnp.float32,
            )
            for odd in range(2)
        ]
        out_ref[w] = jnp.concatenate(parts, axis=1) * SEQ ** (-0.5)


def sketch_own(where, feat_t, mine, other):
    whole = pl.BlockSpec(memory_space=pltpu.VMEM)
    return pl.pallas_call(
        sketch_kernel,
        out_shape=jax.ShapeDtypeStruct((3, K // 2, 2 * K), jnp.float32),
        in_specs=[pl.BlockSpec(memory_space=pltpu.SMEM), whole, whole, whole],
        out_specs=whole,
        scratch_shapes=[pltpu.VMEM((3 * K, SEQ), jnp.float32)],
        compiler_params=pltpu.CompilerParams(vmem_limit_bytes=4 * MIB),
        name="sketch",
    )(where, feat_t, mine, other)


def precond_kernel(row_ref, p_ref, *refs):
    sketches, out_ref, sums = refs[:ROWS], refs[ROWS], refs[ROWS + 1]
    height = p_ref.shape[1]
    lanes = 2 * K
    group = 32

    for w in range(3):

        @pl.loop(0, height // group)
        def _(g):
            at = pl.ds(pl.multiple_of(g * group, group), group)
            totals = [jnp.zeros((group, lanes), jnp.float32) for _ in range(ROWS)]
            for q in range(K // 2):
                part = p_ref[w, at, pl.ds(q * lanes, lanes)]
                for n in range(ROWS):
                    totals[n] = totals[n] + part * sketches[n][w, pl.ds(q, 1), :]
            for n in range(ROWS):
                sums[n, at, :] = totals[n]

        for n in range(ROWS):
            line = jnp.sum(sums[n].T, axis=0, keepdims=True)
            out_ref[w, pl.ds(row_ref[0] ^ n, 1), :] = line


def apply_precond(row, precond, sketches):
    height = precond.shape[1]
    whole = pl.BlockSpec(memory_space=pltpu.VMEM)
    operands = [pltpu.with_memory_space_constraint(a, pltpu.VMEM) for a in [precond, *sketches]]
    return pl.pallas_call(
        precond_kernel,
        out_shape=jax.ShapeDtypeStruct((3, ROWS, height), jnp.float32),
        in_specs=[pl.BlockSpec(memory_space=pltpu.SMEM)] + [whole] * (1 + ROWS),
        out_specs=whole,
        scratch_shapes=[pltpu.VMEM((ROWS, height, 2 * K), jnp.float32)],
        compiler_params=pltpu.CompilerParams(vmem_limit_bytes=4 * MIB),
        name="precond",
    )(row, *operands)


A, C, Y, D = range(4)
INNER = [(t * ROWS + a, t * ROWS + b) for t in range(TENSOR) for a, b in ((1, 2), (2, 1))]
OUTER = [(t * ROWS + a, t * ROWS + b) for t in range(TENSOR) for a, b in ((1, 0), (2, 3))]


def other_core(value):
    return send(value, swap_with(1))


def other_chip(value):
    return send(value, swap_with(2))


def tie(*values):
    return lax.optimization_barrier(values)


def local_split(hidden_in, out_grad, w_gate_up, w_down, feat_proj, unit_proj, precond):
    tensor, row = lax.axis_index("tensor"), lax.axis_index("dp")
    inner = jnp.logical_or(row == 1, row == 2)
    where = jnp.stack([tensor, tensor ^ 1, tensor ^ 2, tensor ^ 3]).astype(jnp.int32)
    row = row.astype(jnp.int32).reshape(1)
    hidden_in, out_grad, where, row, inner = tie(hidden_in, out_grad, where, row, inner)
    step = functools.partial(matmul_step, where)

    own = jnp.stack([hidden_in, out_grad])
    near = send(own, swap_rows(1))
    middle = send(own, INNER)
    own_y = other_chip(own)
    own_c = other_core(own)
    feat_t = jnp.concatenate(
        [
            lax.dot_general(
                feat_proj[:, : 2 * K], hidden_in, (((0,), (1,)), ((), ())), preferred_element_type=jnp.float32
            ),
            lax.dot_general(
                feat_proj[:, 2 * K :], out_grad, (((0,), (1,)), ((), ())), preferred_element_type=jnp.float32
            ),
        ],
        axis=0,
    )
    feat_t = feat_t + other_core(feat_t)
    unit_proj_t = unit_proj.T
    near, middle, own_y, own_c, unit_proj_t, feat_t = tie(near, middle, own_y, own_c, unit_proj_t, feat_t)

    near_c = other_core(near)
    passed = send(middle, OUTER)
    middle_2 = send(near, INNER)
    near_y = other_chip(near)
    own_d = other_core(own_y)
    (acc,) = step([(A, (own, near)), (C, (own_c, near_c))], w_gate_up, w_down)
    passed, middle_2, near_y, own_d, acc = tie(passed, middle_2, near_y, own_d, acc)

    near_d = other_core(near_y)
    third = jnp.where(inner, middle, passed)
    passed_2 = send(middle_2, OUTER)
    third_y = other_chip(third)
    third_c = other_core(third)
    mine_0, theirs_0 = step(
        [(Y, (own_y, near_y)), (D, (own_d, near_d))], w_gate_up, w_down, acc, unit_proj_t
    )
    passed_2, third_y, third_c, mine_0, theirs_0 = tie(passed_2, third_y, third_c, mine_0, theirs_0)

    fourth = jnp.where(inner, middle_2, passed_2)
    fourth_c = other_core(fourth)
    fourth_y = other_chip(fourth)
    third_d = other_core(third_y)
    theirs_0 = other_core(theirs_0)
    (acc,) = step([(A, (third, fourth)), (C, (third_c, fourth_c))], w_gate_up, w_down)
    fourth_y, third_d, mine_0, theirs_0, feat_t, acc = tie(fourth_y, third_d, mine_0, theirs_0, feat_t, acc)

    fourth_d = other_core(fourth_y)
    feat_y = other_chip(feat_t)
    mine_0 = mine_0 + theirs_0
    near_part = send(mine_0[:, SEQ:], swap_rows(1))
    mine_1, theirs_1 = step(
        [(Y, (third_y, fourth_y)), (D, (third_d, fourth_d))], w_gate_up, w_down, acc, unit_proj_t
    )

    near_part, feat_y, mine_1, theirs_1 = tie(near_part, feat_y, mine_1, theirs_1)

    mine_1 = mine_1 + other_core(theirs_1)
    low, high = mine_1[:, :SEQ], mine_1[:, SEQ:]
    part = mine_0[:, :SEQ] + near_part
    feat_t = feat_t + feat_y
    part = part + send(jnp.where(inner, high, low), swap_rows(2)) + send(jnp.where(inner, low, high), swap_rows(3))
    part = part + other_chip(part)
    other = other_core(part)
    sketch = sketch_own(where, feat_t, part, other)
    sketches = [sketch] + [send(sketch, swap_rows(n)) for n in range(1, ROWS)]
    return apply_precond(row, precond, sketches)


def local(hidden_in, out_grad, w_gate_up, w_down, feat_proj, unit_proj, precond):
    fits = (
        lax.axis_size("tensor") == TENSOR
        and lax.axis_size("dp") == ROWS
        and hidden_in.shape[0] == SEQ
        and w_down.shape[0] % 256 == 0
    )
    step = local_split if fits else local_plain
    return step(hidden_in, out_grad, w_gate_up, w_down, feat_proj, unit_proj, precond)


def solution(mesh):
    in_specs = (
        P(("groups", "dp"), "tensor"),
        P(("groups", "dp"), "tensor"),
        P(None, ("tensor", "dp"), None),
        P(("tensor", "dp"), None),
        P("tensor", None),
        P(("tensor", "dp"), None),
        P(None, ("tensor", "dp"), None),
    )
    out_specs = P(None, "groups", ("tensor", "dp"))
    return jax.shard_map(local, mesh=mesh, in_specs=in_specs, out_specs=out_specs, check_vma=False)
```

```python
import functools

import jax
import jax.numpy as jnp
from jax import lax
from jax.experimental import pallas as pl
from jax.experimental.pallas import tpu as pltpu
from jax.sharding import PartitionSpec as P

K = 64
SEQ = 128
BOTH = ("tensor", "dp")
NT = (((1,), (1,)), ((), ()))
MIB = 1 << 20


def project_pair(rows_in, rows_out, columns):
    return jnp.concatenate(
        [
            jnp.dot(rows_in, columns[:, : 2 * K], preferred_element_type=jnp.float32),
            jnp.dot(rows_out, columns[:, 2 * K :], preferred_element_type=jnp.float32),
        ],
        axis=1,
    )


def form_sketch(in_side, out_side):
    seq_count = in_side.shape[0] // SEQ
    left_rows = in_side.reshape(seq_count, SEQ, 3, K)
    right_rows = out_side.reshape(seq_count, SEQ, 3, K)
    sketch = jnp.einsum("stwi,stwj->wsij", left_rows, right_rows, precision=lax.Precision.HIGHEST)
    sketch = sketch * SEQ ** (-0.5)
    return sketch.reshape(3, seq_count, K * K)


def activations(gate_pre, up_pre, hid_grad):
    gate_sig = jax.nn.sigmoid(gate_pre)
    silu_gate = gate_pre * gate_sig
    hidden = (silu_gate * up_pre).astype(jnp.bfloat16)
    gate_grad = (hid_grad * up_pre * gate_sig * (1.0 + gate_pre * (1.0 - gate_sig))).astype(
        jnp.bfloat16
    )
    up_grad = (hid_grad * silu_gate).astype(jnp.bfloat16)
    return gate_grad, up_grad, hidden


def local_plain(hidden_in, out_grad, w_gate_up, w_down, feat_proj, unit_proj, precond):
    unit_width, model_width = w_down.shape
    w_both = w_gate_up.reshape(2 * unit_width, model_width)
    paired = jnp.stack([hidden_in, out_grad])
    columns = lax.all_gather(feat_proj, "tensor", axis=0, tiled=True)
    rows_all = lax.all_gather(paired, "dp", axis=1, tiled=True)
    pieces = lax.all_gather(rows_all, "tensor", axis=2, tiled=True)
    pre_act = lax.dot_general(pieces[0], w_both, NT, preferred_element_type=jnp.float32)
    hid_grad = lax.dot_general(pieces[1], w_down, NT, preferred_element_type=jnp.float32)
    feat_side = project_pair(pieces[0], pieces[1], columns)
    sides = activations(pre_act[:, :unit_width], pre_act[:, unit_width:], hid_grad)
    unit_part = jnp.concatenate(
        [
            jnp.dot(side, unit_proj[:, n * K : (n + 1) * K], preferred_element_type=jnp.float32)
            for n, side in enumerate(sides)
        ],
        axis=1,
    )
    unit_side = lax.psum(unit_part, BOTH)
    in_side = jnp.concatenate([feat_side[:, : 2 * K], unit_side[:, 2 * K :]], axis=1)
    out_side = jnp.concatenate([unit_side[:, : 2 * K], feat_side[:, 2 * K :]], axis=1)
    sketch = form_sketch(in_side, out_side)
    return jnp.einsum("wrc,wsc->wsr", precond, sketch, precision=lax.Precision.HIGHEST)


TENSOR = 4
ROWS = 4


def swap_with(flip):
    return [(t * ROWS + z, (t ^ flip) * ROWS + z) for t in range(TENSOR) for z in range(ROWS)]


def swap_rows(flip):
    return [(t * ROWS + z, t * ROWS + (z ^ flip)) for t in range(TENSOR) for z in range(ROWS)]


def send(value, pairs):
    return lax.ppermute(value, BOTH, pairs)


def matmul_kernel(count, last, *refs):
    refs = list(refs)
    where_ref = refs.pop(0)
    pieces = [(refs.pop(0), refs.pop(0)) for _ in range(count)]
    gate_up = [refs.pop(0) for _ in range(count)]
    down = [refs.pop(0) for _ in range(count)]
    if last:
        acc_in, proj_ref, mine_ref, theirs_ref = (refs.pop(0) for _ in range(4))
    else:
        acc_out = refs.pop(0)
    rows = [refs.pop(0) for _ in range(count)]
    sems = refs.pop(0)
    step = pl.program_id(0)

    @pl.when(step == 0)
    def _():
        copies = []
        for n in range(count):
            at = 0
            for m, piece in enumerate(pieces[n]):
                target = rows[n].at[:, pl.ds(at, piece.shape[1]), :]
                copies.append(pltpu.make_async_copy(piece, target, sems.at[2 * n + m]))
                at += piece.shape[1]
        for copy in copies:
            copy.start()
        for copy in copies:
            copy.wait()

    def total(which):
        value = acc_in[step, which] if last else None
        for n in range(count):
            weight = down[n][...] if which == 2 else gate_up[n][which]
            part = lax.dot_general(
                rows[n][1 if which == 2 else 0], weight, NT, preferred_element_type=jnp.float32
            )
            value = part if value is None else value + part
        return value

    if not last:
        for which in range(3):
            acc_out[step, which] = total(which)
        return
    ut_ref = refs.pop(0)

    @pl.when(step == 0)
    def _():
        ut_ref[...] = jnp.zeros_like(ut_ref)

    sides = activations(total(0), total(1), total(2))
    for n, side in enumerate(sides):
        ut_ref[pl.ds(n * K, K), :] += lax.dot_general(
            proj_ref[pl.ds(n * K, K), :], side, NT, preferred_element_type=jnp.float32
        )

    @pl.when(step == pl.num_programs(0) - 1)
    def _():
        half = mine_ref.shape[0]
        core = lax.rem(where_ref[0], 2)
        mine_ref[...] = ut_ref[pl.ds(pl.multiple_of(core * half, 8), half), :]
        theirs_ref[...] = ut_ref[pl.ds(pl.multiple_of((1 - core) * half, 8), half), :]


def matmul_step(where, blocks, w_gate_up, w_down, acc=None, unit_proj_t=None):
    last = acc is not None
    count = len(blocks)
    unit_width = w_down.shape[0]
    width = blocks[0][1][0].shape[2]
    tokens = sum(piece.shape[1] for piece in blocks[0][1])
    tile = 256
    tiles = unit_width // tile
    whole = pl.BlockSpec(memory_space=pltpu.VMEM)

    in_specs, operands = [], []
    for _, pieces in blocks:
        for piece in pieces:
            in_specs.append(whole)
            operands.append(pltpu.with_memory_space_constraint(piece, pltpu.VMEM))
    for owner, _ in blocks:
        in_specs.append(pl.BlockSpec((2, tile, width), lambda i, r, o=owner: (0, i, r[o])))
        operands.append(pltpu.with_memory_space_constraint(w_gate_up, pltpu.HBM))
    for owner, _ in blocks:
        in_specs.append(pl.BlockSpec((tile, width), lambda i, r, o=owner: (i, r[o])))
        operands.append(pltpu.with_memory_space_constraint(w_down, pltpu.HBM))
    need = count * width * (2 * tokens + 2 * 3 * tile) * 2 + 4 * MIB
    scratch = [pltpu.VMEM((2, tokens, width), jnp.bfloat16) for _ in blocks]
    scratch.append(pltpu.SemaphoreType.DMA((2 * count,)))
    if last:
        in_specs.append(whole)
        operands.append(pltpu.with_memory_space_constraint(acc, pltpu.VMEM))
        out_shape, out_specs = [], []
    else:
        out_shape, out_specs = [pltpu.VMEM((tiles, 3, tokens, tile), jnp.float32)], [whole]
    if last:
        in_specs.append(pl.BlockSpec((3 * K, tile), lambda i, r: (0, i)))
        operands.append(unit_proj_t)
        half = jax.ShapeDtypeStruct((3 * K // 2, tokens), jnp.float32)
        out_shape += [half] * 2
        out_specs += [pl.BlockSpec(half.shape, lambda i, r: (0, 0))] * 2
        scratch.append(pltpu.VMEM((3 * K, tokens), jnp.float32))
        need += 4 * MIB
    return pl.pallas_call(
        functools.partial(matmul_kernel, count, last),
        out_shape=out_shape,
        grid_spec=pltpu.PrefetchScalarGridSpec(
            num_scalar_prefetch=1,
            grid=(tiles,),
            in_specs=in_specs,
            out_specs=out_specs,
            scratch_shapes=scratch,
        ),
        compiler_params=pltpu.CompilerParams(vmem_limit_bytes=need),
        cost_estimate=pl.CostEstimate(
            flops=2 * tokens * 3 * unit_width * width * count,
            bytes_accessed=3 * unit_width * width * count * 2,
            transcendentals=0,
        ),
        name="matmul",
    )(where, *operands)


def sketch_kernel(where_ref, feat_ref, mine_ref, other_ref, out_ref, unit_ref):
    half = mine_ref.shape[0]
    core = lax.rem(where_ref[0], 2)
    unit_ref[pl.ds(pl.multiple_of(core * half, 8), half), :] = mine_ref[...]
    unit_ref[pl.ds(pl.multiple_of((1 - core) * half, 8), half), :] = other_ref[...]
    for w in range(3):
        in_ref, side_ref = (feat_ref, unit_ref) if w < 2 else (unit_ref, feat_ref)
        right = side_ref[pl.ds(w * K, K), :]
        parts = [
            lax.dot_general(
                in_ref[pl.ds(w * K + odd, K // 2, stride=2), :],
                right,
                NT,
                precision=lax.Precision.HIGHEST,
                preferred_element_type=jnp.float32,
            )
            for odd in range(2)
        ]
        out_ref[w] = jnp.concatenate(parts, axis=1) * SEQ ** (-0.5)


def sketch_own(where, feat_t, mine, other):
    whole = pl.BlockSpec(memory_space=pltpu.VMEM)
    return pl.pallas_call(
        sketch_kernel,
        out_shape=jax.ShapeDtypeStruct((3, K // 2, 2 * K), jnp.float32),
        in_specs=[pl.BlockSpec(memory_space=pltpu.SMEM), whole, whole, whole],
        out_specs=whole,
        scratch_shapes=[pltpu.VMEM((3 * K, SEQ), jnp.float32)],
        compiler_params=pltpu.CompilerParams(vmem_limit_bytes=4 * MIB),
        name="sketch",
    )(where, feat_t, mine, other)


def precond_kernel(flips, row_ref, p_ref, *refs):
    count = len(flips)
    sketches, refs = refs[:count], refs[count:]
    if count < ROWS and 0 not in flips:
        own_ref, out_ref, sums = refs
        out_ref[:, pl.ds(row_ref[0], 1), :] = own_ref[...]
    else:
        out_ref, sums = refs
    height = p_ref.shape[1]
    lanes = 2 * K
    group = 32

    for w in range(3):

        @pl.loop(0, height // group)
        def _(g):
            at = pl.ds(pl.multiple_of(g * group, group), group)
            totals = [jnp.zeros((group, lanes), jnp.float32) for _ in range(count)]
            for q in range(K // 2):
                part = p_ref[w, at, pl.ds(q * lanes, lanes)]
                for n in range(count):
                    totals[n] = totals[n] + part * sketches[n][w, pl.ds(q, 1), :]
            for n in range(count):
                sums[n, at, :] = totals[n]

        for n in range(count):
            line = jnp.sum(sums[n].T, axis=0, keepdims=True)
            if out_ref.shape[1] == 1:
                out_ref[w] = line
            else:
                out_ref[w, pl.ds(row_ref[0] ^ flips[n], 1), :] = line


def apply_precond(row, precond, sketches, flips, own=None):
    height = precond.shape[1]
    whole = pl.BlockSpec(memory_space=pltpu.VMEM)
    operands = [precond, *sketches] + ([] if own is None else [own])
    operands = [pltpu.with_memory_space_constraint(a, pltpu.VMEM) for a in operands]
    return pl.pallas_call(
        functools.partial(precond_kernel, flips),
        out_shape=jax.ShapeDtypeStruct((3, 1 if own is None else ROWS, height), jnp.float32),
        in_specs=[pl.BlockSpec(memory_space=pltpu.SMEM)] + [whole] * len(operands),
        out_specs=whole,
        scratch_shapes=[pltpu.VMEM((len(flips), height, 2 * K), jnp.float32)],
        compiler_params=pltpu.CompilerParams(vmem_limit_bytes=4 * MIB),
        name="precond",
    )(row, *operands)


A, C, Y, D = range(4)
INNER = [(t * ROWS + a, t * ROWS + b) for t in range(TENSOR) for a, b in ((1, 2), (2, 1))]
OUTER = [(t * ROWS + a, t * ROWS + b) for t in range(TENSOR) for a, b in ((1, 0), (2, 3))]


def other_core(value):
    return send(value, swap_with(1))


def other_chip(value):
    return send(value, swap_with(2))


def tie(*values):
    return lax.optimization_barrier(values)


def local_split(hidden_in, out_grad, w_gate_up, w_down, feat_proj, unit_proj, precond):
    tensor, row = lax.axis_index("tensor"), lax.axis_index("dp")
    inner = jnp.logical_or(row == 1, row == 2)
    where = jnp.stack([tensor, tensor ^ 1, tensor ^ 2, tensor ^ 3]).astype(jnp.int32)
    row = row.astype(jnp.int32).reshape(1)
    hidden_in, out_grad, where, row, inner = tie(hidden_in, out_grad, where, row, inner)
    step = functools.partial(matmul_step, where)

    own = jnp.stack([hidden_in, out_grad])
    near = send(own, swap_rows(1))
    middle = send(own, INNER)
    own_y = other_chip(own)
    own_c = other_core(own)
    feat_t = jnp.concatenate(
        [
            lax.dot_general(
                feat_proj[:, : 2 * K], hidden_in, (((0,), (1,)), ((), ())), preferred_element_type=jnp.float32
            ),
            lax.dot_general(
                feat_proj[:, 2 * K :], out_grad, (((0,), (1,)), ((), ())), preferred_element_type=jnp.float32
            ),
        ],
        axis=0,
    )
    feat_t = feat_t + other_core(feat_t)
    unit_proj_t = unit_proj.T
    near, middle, own_y, own_c, unit_proj_t, feat_t = tie(near, middle, own_y, own_c, unit_proj_t, feat_t)

    near_c = other_core(near)
    passed = send(middle, OUTER)
    middle_2 = send(near, INNER)
    near_y = other_chip(near)
    own_d = other_core(own_y)
    (acc,) = step([(A, (own, near)), (C, (own_c, near_c))], w_gate_up, w_down)
    passed, middle_2, near_y, own_d, feat_t, acc = tie(passed, middle_2, near_y, own_d, feat_t, acc)
    feat_y = other_chip(feat_t)

    near_d = other_core(near_y)
    third = jnp.where(inner, middle, passed)
    passed_2 = send(middle_2, OUTER)
    third_y = other_chip(third)
    third_c = other_core(third)
    mine_0, theirs_0 = step(
        [(Y, (own_y, near_y)), (D, (own_d, near_d))], w_gate_up, w_down, acc, unit_proj_t
    )
    passed_2, third_y, third_c, mine_0, theirs_0, feat_y = tie(
        passed_2, third_y, third_c, mine_0, theirs_0, feat_y
    )
    feat_t = feat_t + feat_y

    fourth = jnp.where(inner, middle_2, passed_2)
    fourth_c = other_core(fourth)
    fourth_y = other_chip(fourth)
    third_d = other_core(third_y)
    theirs_0 = other_core(theirs_0)
    (acc,) = step([(A, (third, fourth)), (C, (third_c, fourth_c))], w_gate_up, w_down)
    fourth_y, third_d, mine_0, theirs_0, feat_t, acc = tie(fourth_y, third_d, mine_0, theirs_0, feat_t, acc)

    fourth_d = other_core(fourth_y)
    mine_0 = mine_0 + theirs_0
    near_part = send(mine_0[:, SEQ:], swap_rows(1))
    mine_1, theirs_1 = step(
        [(Y, (third_y, fourth_y)), (D, (third_d, fourth_d))], w_gate_up, w_down, acc, unit_proj_t
    )

    near_part, mine_1, theirs_1 = tie(near_part, mine_1, theirs_1)

    mine_1 = mine_1 + other_core(theirs_1)
    low, high = mine_1[:, :SEQ], mine_1[:, SEQ:]
    part = mine_0[:, :SEQ] + near_part
    part = part + send(jnp.where(inner, high, low), swap_rows(2)) + send(jnp.where(inner, low, high), swap_rows(3))
    part = part + other_chip(part)
    other = other_core(part)
    sketch = sketch_own(where, feat_t, part, other)
    sketches = [send(sketch, swap_rows(n)) for n in range(1, ROWS)]
    own_line = apply_precond(row, precond, [sketch], (0,))
    sketches, own_line = tie(sketches, own_line)
    return apply_precond(row, precond, sketches, (1, 2, 3), own_line)


def local(hidden_in, out_grad, w_gate_up, w_down, feat_proj, unit_proj, precond):
    fits = (
        lax.axis_size("tensor") == TENSOR
        and lax.axis_size("dp") == ROWS
        and hidden_in.shape[0] == SEQ
        and w_down.shape[0] % 256 == 0
    )
    step = local_split if fits else local_plain
    return step(hidden_in, out_grad, w_gate_up, w_down, feat_proj, unit_proj, precond)


def solution(mesh):
    in_specs = (
        P(("groups", "dp"), "tensor"),
        P(("groups", "dp"), "tensor"),
        P(None, ("tensor", "dp"), None),
        P(("tensor", "dp"), None),
        P("tensor", None),
        P(("tensor", "dp"), None),
        P(None, ("tensor", "dp"), None),
    )
    out_specs = P(None, "groups", ("tensor", "dp"))
    return jax.shard_map(local, mesh=mesh, in_specs=in_specs, out_specs=out_specs, check_vma=False)
```

```python
import functools

import jax
import jax.numpy as jnp
from jax import lax
from jax.experimental import pallas as pl
from jax.experimental.pallas import tpu as pltpu
from jax.sharding import PartitionSpec as P

K = 64
SEQ = 128
BOTH = ("tensor", "dp")
NT = (((1,), (1,)), ((), ()))
MIB = 1 << 20


def project_pair(rows_in, rows_out, columns):
    return jnp.concatenate(
        [
            jnp.dot(rows_in, columns[:, : 2 * K], preferred_element_type=jnp.float32),
            jnp.dot(rows_out, columns[:, 2 * K :], preferred_element_type=jnp.float32),
        ],
        axis=1,
    )


def form_sketch(in_side, out_side):
    seq_count = in_side.shape[0] // SEQ
    left_rows = in_side.reshape(seq_count, SEQ, 3, K)
    right_rows = out_side.reshape(seq_count, SEQ, 3, K)
    sketch = jnp.einsum("stwi,stwj->wsij", left_rows, right_rows, precision=lax.Precision.HIGHEST)
    sketch = sketch * SEQ ** (-0.5)
    return sketch.reshape(3, seq_count, K * K)


def activations(gate_pre, up_pre, hid_grad):
    gate_sig = jax.nn.sigmoid(gate_pre)
    silu_gate = gate_pre * gate_sig
    hidden = (silu_gate * up_pre).astype(jnp.bfloat16)
    gate_grad = (hid_grad * up_pre * gate_sig * (1.0 + gate_pre * (1.0 - gate_sig))).astype(
        jnp.bfloat16
    )
    up_grad = (hid_grad * silu_gate).astype(jnp.bfloat16)
    return gate_grad, up_grad, hidden


def local_plain(hidden_in, out_grad, w_gate_up, w_down, feat_proj, unit_proj, precond):
    unit_width, model_width = w_down.shape
    w_both = w_gate_up.reshape(2 * unit_width, model_width)
    paired = jnp.stack([hidden_in, out_grad])
    columns = lax.all_gather(feat_proj, "tensor", axis=0, tiled=True)
    rows_all = lax.all_gather(paired, "dp", axis=1, tiled=True)
    pieces = lax.all_gather(rows_all, "tensor", axis=2, tiled=True)
    pre_act = lax.dot_general(pieces[0], w_both, NT, preferred_element_type=jnp.float32)
    hid_grad = lax.dot_general(pieces[1], w_down, NT, preferred_element_type=jnp.float32)
    feat_side = project_pair(pieces[0], pieces[1], columns)
    sides = activations(pre_act[:, :unit_width], pre_act[:, unit_width:], hid_grad)
    unit_part = jnp.concatenate(
        [
            jnp.dot(side, unit_proj[:, n * K : (n + 1) * K], preferred_element_type=jnp.float32)
            for n, side in enumerate(sides)
        ],
        axis=1,
    )
    unit_side = lax.psum(unit_part, BOTH)
    in_side = jnp.concatenate([feat_side[:, : 2 * K], unit_side[:, 2 * K :]], axis=1)
    out_side = jnp.concatenate([unit_side[:, : 2 * K], feat_side[:, 2 * K :]], axis=1)
    sketch = form_sketch(in_side, out_side)
    return jnp.einsum("wrc,wsc->wsr", precond, sketch, precision=lax.Precision.HIGHEST)


TENSOR = 4
ROWS = 4


def swap_with(flip):
    return [(t * ROWS + z, (t ^ flip) * ROWS + z) for t in range(TENSOR) for z in range(ROWS)]


def swap_rows(flip):
    return [(t * ROWS + z, t * ROWS + (z ^ flip)) for t in range(TENSOR) for z in range(ROWS)]


def send(value, pairs):
    return lax.ppermute(value, BOTH, pairs)


def matmul_kernel(count, last, *refs):
    refs = list(refs)
    where_ref = refs.pop(0)
    pieces = [(refs.pop(0), refs.pop(0)) for _ in range(count)]
    gate_up = [refs.pop(0) for _ in range(count)]
    down = [refs.pop(0) for _ in range(count)]
    if last:
        acc_in, proj_ref, mine_ref, theirs_ref = (refs.pop(0) for _ in range(4))
    else:
        acc_out = refs.pop(0)
    rows = [refs.pop(0) for _ in range(count)]
    sems = refs.pop(0)
    step = pl.program_id(0)

    def copies(n):
        at, made = 0, []
        for m, piece in enumerate(pieces[n]):
            target = rows[n].at[:, pl.ds(at, piece.shape[1]), :]
            made.append(pltpu.make_async_copy(piece, target, sems.at[2 * n + m]))
            at += piece.shape[1]
        return made

    @pl.when(step == 0)
    def _():
        for n in range(count):
            for copy in copies(n):
                copy.start()

    def arrive(n):
        @pl.when(step == 0)
        def _():
            for copy in copies(n):
                copy.wait()

    def total(which):
        value = acc_in[step, which] if last else None
        for n in range(count):
            if which == 0:
                arrive(n)
            weight = down[n][...] if which == 2 else gate_up[n][which]
            part = lax.dot_general(
                rows[n][1 if which == 2 else 0], weight, NT, preferred_element_type=jnp.float32
            )
            value = part if value is None else value + part
        return value

    if not last:
        for which in range(3):
            acc_out[step, which] = total(which)
        return
    ut_ref = refs.pop(0)

    @pl.when(step == 0)
    def _():
        ut_ref[...] = jnp.zeros_like(ut_ref)

    sides = activations(total(0), total(1), total(2))
    for n, side in enumerate(sides):
        ut_ref[pl.ds(n * K, K), :] += lax.dot_general(
            proj_ref[pl.ds(n * K, K), :], side, NT, preferred_element_type=jnp.float32
        )

    @pl.when(step == pl.num_programs(0) - 1)
    def _():
        half = mine_ref.shape[0]
        core = lax.rem(where_ref[0], 2)
        mine_ref[...] = ut_ref[pl.ds(pl.multiple_of(core * half, 8), half), :]
        theirs_ref[...] = ut_ref[pl.ds(pl.multiple_of((1 - core) * half, 8), half), :]


def matmul_step(where, blocks, w_gate_up, w_down, acc=None, unit_proj_t=None):
    last = acc is not None
    count = len(blocks)
    unit_width = w_down.shape[0]
    width = blocks[0][1][0].shape[2]
    tokens = sum(piece.shape[1] for piece in blocks[0][1])
    tile = 256
    tiles = unit_width // tile
    whole = pl.BlockSpec(memory_space=pltpu.VMEM)

    in_specs, operands = [], []
    for _, pieces in blocks:
        for piece in pieces:
            in_specs.append(whole)
            operands.append(pltpu.with_memory_space_constraint(piece, pltpu.VMEM))
    for owner, _ in blocks:
        in_specs.append(pl.BlockSpec((2, tile, width), lambda i, r, o=owner: (0, i, r[o])))
        operands.append(pltpu.with_memory_space_constraint(w_gate_up, pltpu.HBM))
    for owner, _ in blocks:
        in_specs.append(pl.BlockSpec((tile, width), lambda i, r, o=owner: (i, r[o])))
        operands.append(pltpu.with_memory_space_constraint(w_down, pltpu.HBM))
    need = count * width * (2 * tokens + 2 * 3 * tile) * 2 + 4 * MIB
    scratch = [pltpu.VMEM((2, tokens, width), jnp.bfloat16) for _ in blocks]
    scratch.append(pltpu.SemaphoreType.DMA((2 * count,)))
    if last:
        in_specs.append(whole)
        operands.append(pltpu.with_memory_space_constraint(acc, pltpu.VMEM))
        out_shape, out_specs = [], []
    else:
        out_shape, out_specs = [pltpu.VMEM((tiles, 3, tokens, tile), jnp.float32)], [whole]
    if last:
        in_specs.append(pl.BlockSpec((3 * K, tile), lambda i, r: (0, i)))
        operands.append(unit_proj_t)
        half = jax.ShapeDtypeStruct((3 * K // 2, tokens), jnp.float32)
        out_shape += [half] * 2
        out_specs += [pl.BlockSpec(half.shape, lambda i, r: (0, 0))] * 2
        scratch.append(pltpu.VMEM((3 * K, tokens), jnp.float32))
        need += 4 * MIB
    return pl.pallas_call(
        functools.partial(matmul_kernel, count, last),
        out_shape=out_shape,
        grid_spec=pltpu.PrefetchScalarGridSpec(
            num_scalar_prefetch=1,
            grid=(tiles,),
            in_specs=in_specs,
            out_specs=out_specs,
            scratch_shapes=scratch,
        ),
        compiler_params=pltpu.CompilerParams(vmem_limit_bytes=need),
        cost_estimate=pl.CostEstimate(
            flops=2 * tokens * 3 * unit_width * width * count,
            bytes_accessed=3 * unit_width * width * count * 2,
            transcendentals=0,
        ),
        name="matmul",
    )(where, *operands)


def sketch_kernel(where_ref, feat_ref, mine_ref, other_ref, out_ref, unit_ref):
    half = mine_ref.shape[0]
    core = lax.rem(where_ref[0], 2)
    unit_ref[pl.ds(pl.multiple_of(core * half, 8), half), :] = mine_ref[...]
    unit_ref[pl.ds(pl.multiple_of((1 - core) * half, 8), half), :] = other_ref[...]
    for w in range(3):
        in_ref, side_ref = (feat_ref, unit_ref) if w < 2 else (unit_ref, feat_ref)
        right = side_ref[pl.ds(w * K, K), :]
        parts = [
            lax.dot_general(
                in_ref[pl.ds(w * K + odd, K // 2, stride=2), :],
                right,
                NT,
                precision=lax.Precision.HIGHEST,
                preferred_element_type=jnp.float32,
            )
            for odd in range(2)
        ]
        out_ref[w] = jnp.concatenate(parts, axis=1) * SEQ ** (-0.5)


def sketch_own(where, feat_t, mine, other):
    whole = pl.BlockSpec(memory_space=pltpu.VMEM)
    return pl.pallas_call(
        sketch_kernel,
        out_shape=jax.ShapeDtypeStruct((3, K // 2, 2 * K), jnp.float32),
        in_specs=[pl.BlockSpec(memory_space=pltpu.SMEM), whole, whole, whole],
        out_specs=whole,
        scratch_shapes=[pltpu.VMEM((3 * K, SEQ), jnp.float32)],
        compiler_params=pltpu.CompilerParams(vmem_limit_bytes=4 * MIB),
        name="sketch",
    )(where, feat_t, mine, other)


def precond_kernel(flips, row_ref, p_ref, *refs):
    count = len(flips)
    sketches, refs = refs[:count], refs[count:]
    if count < ROWS and 0 not in flips:
        own_ref, out_ref, sums = refs
        out_ref[:, pl.ds(row_ref[0], 1), :] = own_ref[...]
    else:
        out_ref, sums = refs
    height = p_ref.shape[1]
    lanes = 2 * K
    group = 32

    for w in range(3):

        @pl.loop(0, height // group)
        def _(g):
            at = pl.ds(pl.multiple_of(g * group, group), group)
            totals = [jnp.zeros((group, lanes), jnp.float32) for _ in range(count)]
            for q in range(K // 2):
                part = p_ref[w, at, pl.ds(q * lanes, lanes)]
                for n in range(count):
                    totals[n] = totals[n] + part * sketches[n][w, pl.ds(q, 1), :]
            for n in range(count):
                sums[n, at, :] = totals[n]

        for n in range(count):
            line = jnp.sum(sums[n].T, axis=0, keepdims=True)
            if out_ref.shape[1] == 1:
                out_ref[w] = line
            else:
                out_ref[w, pl.ds(row_ref[0] ^ flips[n], 1), :] = line


def apply_precond(row, precond, sketches, flips, own=None):
    height = precond.shape[1]
    whole = pl.BlockSpec(memory_space=pltpu.VMEM)
    operands = [precond, *sketches] + ([] if own is None else [own])
    operands = [pltpu.with_memory_space_constraint(a, pltpu.VMEM) for a in operands]
    return pl.pallas_call(
        functools.partial(precond_kernel, flips),
        out_shape=jax.ShapeDtypeStruct((3, 1 if own is None else ROWS, height), jnp.float32),
        in_specs=[pl.BlockSpec(memory_space=pltpu.SMEM)] + [whole] * len(operands),
        out_specs=whole,
        scratch_shapes=[pltpu.VMEM((len(flips), height, 2 * K), jnp.float32)],
        compiler_params=pltpu.CompilerParams(vmem_limit_bytes=4 * MIB),
        name="precond",
    )(row, *operands)


A, C, Y, D = range(4)
INNER = [(t * ROWS + a, t * ROWS + b) for t in range(TENSOR) for a, b in ((1, 2), (2, 1))]
OUTER = [(t * ROWS + a, t * ROWS + b) for t in range(TENSOR) for a, b in ((1, 0), (2, 3))]


def other_core(value):
    return send(value, swap_with(1))


def other_chip(value):
    return send(value, swap_with(2))


def tie(*values):
    return lax.optimization_barrier(values)


def local_split(hidden_in, out_grad, w_gate_up, w_down, feat_proj, unit_proj, precond):
    tensor, row = lax.axis_index("tensor"), lax.axis_index("dp")
    inner = jnp.logical_or(row == 1, row == 2)
    where = jnp.stack([tensor, tensor ^ 1, tensor ^ 2, tensor ^ 3]).astype(jnp.int32)
    row = row.astype(jnp.int32).reshape(1)
    hidden_in, out_grad, where, row, inner = tie(hidden_in, out_grad, where, row, inner)
    step = functools.partial(matmul_step, where)

    own = jnp.stack([hidden_in, out_grad])
    near = send(own, swap_rows(1))
    middle = send(own, INNER)
    own_y = other_chip(own)
    own_c = other_core(own)
    feat_t = jnp.concatenate(
        [
            lax.dot_general(
                feat_proj[:, : 2 * K], hidden_in, (((0,), (1,)), ((), ())), preferred_element_type=jnp.float32
            ),
            lax.dot_general(
                feat_proj[:, 2 * K :], out_grad, (((0,), (1,)), ((), ())), preferred_element_type=jnp.float32
            ),
        ],
        axis=0,
    )
    feat_t = feat_t + other_core(feat_t)
    unit_proj_t = unit_proj.T
    near, middle, own_y, own_c, unit_proj_t, feat_t = tie(near, middle, own_y, own_c, unit_proj_t, feat_t)

    near_c = other_core(near)
    passed = send(middle, OUTER)
    middle_2 = send(near, INNER)
    near_y = other_chip(near)
    own_d = other_core(own_y)
    (acc,) = step([(A, (own, near)), (C, (own_c, near_c))], w_gate_up, w_down)
    passed, middle_2, near_y, own_d, feat_t, acc = tie(passed, middle_2, near_y, own_d, feat_t, acc)
    feat_y = other_chip(feat_t)

    near_d = other_core(near_y)
    third = jnp.where(inner, middle, passed)
    passed_2 = send(middle_2, OUTER)
    third_y = other_chip(third)
    third_c = other_core(third)
    mine_0, theirs_0 = step(
        [(Y, (own_y, near_y)), (D, (own_d, near_d))], w_gate_up, w_down, acc, unit_proj_t
    )
    passed_2, third_y, third_c, mine_0, theirs_0, feat_y = tie(
        passed_2, third_y, third_c, mine_0, theirs_0, feat_y
    )
    feat_t = feat_t + feat_y

    fourth = jnp.where(inner, middle_2, passed_2)
    fourth_c = other_core(fourth)
    fourth_y = other_chip(fourth)
    third_d = other_core(third_y)
    theirs_0 = other_core(theirs_0)
    (acc,) = step([(A, (third, fourth)), (C, (third_c, fourth_c))], w_gate_up, w_down)
    fourth_y, third_d, mine_0, theirs_0, feat_t, acc = tie(fourth_y, third_d, mine_0, theirs_0, feat_t, acc)

    fourth_d = other_core(fourth_y)
    mine_0 = mine_0 + theirs_0
    near_part = send(mine_0[:, SEQ:], swap_rows(1))
    mine_1, theirs_1 = step(
        [(Y, (third_y, fourth_y)), (D, (third_d, fourth_d))], w_gate_up, w_down, acc, unit_proj_t
    )

    near_part, mine_1, theirs_1 = tie(near_part, mine_1, theirs_1)

    mine_1 = mine_1 + other_core(theirs_1)
    low, high = mine_1[:, :SEQ], mine_1[:, SEQ:]
    part = mine_0[:, :SEQ] + near_part
    part = part + send(jnp.where(inner, high, low), swap_rows(2)) + send(jnp.where(inner, low, high), swap_rows(3))
    part = part + other_chip(part)
    other = other_core(part)
    sketch = sketch_own(where, feat_t, part, other)
    sketches = [send(sketch, swap_rows(n)) for n in range(1, ROWS)]
    own_line = apply_precond(row, precond, [sketch], (0,))
    sketches, own_line = tie(sketches, own_line)
    return apply_precond(row, precond, sketches, (1, 2, 3), own_line)


def local(hidden_in, out_grad, w_gate_up, w_down, feat_proj, unit_proj, precond):
    fits = (
        lax.axis_size("tensor") == TENSOR
        and lax.axis_size("dp") == ROWS
        and hidden_in.shape[0] == SEQ
        and w_down.shape[0] % 256 == 0
    )
    step = local_split if fits else local_plain
    return step(hidden_in, out_grad, w_gate_up, w_down, feat_proj, unit_proj, precond)


def solution(mesh):
    in_specs = (
        P(("groups", "dp"), "tensor"),
        P(("groups", "dp"), "tensor"),
        P(None, ("tensor", "dp"), None),
        P(("tensor", "dp"), None),
        P("tensor", None),
        P(("tensor", "dp"), None),
        P(None, ("tensor", "dp"), None),
    )
    out_specs = P(None, "groups", ("tensor", "dp"))
    return jax.shard_map(local, mesh=mesh, in_specs=in_specs, out_specs=out_specs, check_vma=False)
```
